32 devices in a mesh: rep: 2 (over x), fsdp: 16 (over z, y, core).
Axes of the slice: x: 2, y: 2, z: 4, core: 2. Of those that a mesh axis runs over, the one named last changes fastest.
Arguments:
- input_short: bfloat16 [128, 128, 768], P(('rep', 'fsdp')), may hold values from -6 to 6
- input_long: bfloat16 [64, 256, 768], P(('rep', 'fsdp')), may hold values from -6 to 6
- steps_short: int32 [128], P(('rep', 'fsdp')), may hold values from 0 to 999
- steps_long: int32 [64], P(('rep', 'fsdp')), may hold values from 0 to 999
- upstream_short: bfloat16 [128, 128, 768], P(('rep', 'fsdp')), may hold values from -6 to 6
- upstream_long: bfloat16 [64, 256, 768], P(('rep', 'fsdp')), may hold values from -6 to 6
- step_table: float32 [1000, 768], P(None, 'fsdp'), may hold values from -3 to 3
- attn_gain: float32 [768], P('fsdp'), may hold values from 0.5 to 1.5
- attn_shift: float32 [768], P('fsdp'), may hold values from -2 to 2
- qkv_weight: float32 [768, 2304], P('fsdp'), may hold values from -0.21875 to 0.21875
- query_bias: float32 [768], P('fsdp'), may hold values from -2 to 2
- value_bias: float32 [768], P('fsdp'), may hold values from -2 to 2
- out_weight: float32 [768, 768], P('fsdp'), may hold values from -0.625 to 0.625
- out_bias: float32 [768], P('fsdp'), may hold values from -2 to 2
- ffn_gain: float32 [768], P('fsdp'), may hold values from 0.5 to 1.5
- ffn_shift: float32 [768], P('fsdp'), may hold values from -2 to 2
- up_weight: float32 [768, 3072], P('fsdp'), may hold values from -0.21875 to 0.21875
- up_bias: float32 [3072], P('fsdp'), may hold values from -2 to 2
- down_weight: float32 [3072, 768], P('fsdp'), may hold values from -0.15625 to 0.15625
- down_bias: float32 [768], P('fsdp'), may hold values from -2 to 2
Outputs:
- output_short: bfloat16 [128, 128, 768], P(('rep', 'fsdp'))
- output_long: bfloat16 [64, 256, 768], P(('rep', 'fsdp'))
- input_grad_short: bfloat16 [128, 128, 768], P(('rep', 'fsdp'))
- input_grad_long: bfloat16 [64, 256, 768], P(('rep', 'fsdp'))
- table_grad: float32 [1000, 768], P(None, 'fsdp')
- attn_gain_grad: float32 [768], P('fsdp')
- attn_shift_grad: float32 [768], P('fsdp')
- qkv_weight_grad: float32 [768, 2304], P('fsdp')
- query_bias_grad: float32 [768], P('fsdp')
- value_bias_grad: float32 [768], P('fsdp')
- out_weight_grad: float32 [768, 768], P('fsdp')
- out_bias_grad: float32 [768], P('fsdp')
- ffn_gain_grad: float32 [768], P('fsdp')
- ffn_shift_grad: float32 [768], P('fsdp')
- up_weight_grad: float32 [768, 3072], P('fsdp')
- up_bias_grad: float32 [3072], P('fsdp')
- down_weight_grad: float32 [3072, 768], P('fsdp')
- down_bias_grad: float32 [768], P('fsdp')
The draws below stay inside these ranges and needn't reach their ends.
All inputs are finite; a program needn't handle non-finite values.
Results may differ from the reference program's by a relative error of at most 0.014.
Values may be sent and summed in bfloat16 or wider, within the bound.
No kernel may reach another device: no remote copies, remote signals or barrier semaphores. Data moves between devices by JAX's collectives and lax.ppermute only.
A program may use at most 192 MiB of HBM per device.

```python
import jax
import jax.numpy as jnp
from jax import lax

D = 768
HEADS = 12
HEAD_DIM = 64
FF = 3072
TIMESTEPS = 1000
LEN_S = 128
LEN_L = 256
SHORTS = 128
LONGS = 64


def with_ends(drawn, key, low, top_value):
    dims = drawn.shape
    place = [jax.random.randint(jax.random.fold_in(key, axis), (), 0, dims[axis]) for axis in range(len(dims))]
    drawn = drawn.at[tuple(place)].set(low)
    longest = dims.index(max(dims))
    place[longest] = (place[longest] + 1) % dims[longest]
    return drawn.at[tuple(place)].set(top_value)


def raised(values, stream_key, source, target, shards_of, factor):
    def block_of(dim):
        return (jnp.arange(values.shape[dim]) // (values.shape[dim] // shards_of)).reshape((-1,) + (1,) * (values.ndim - 1 - dim))

    near = jax.random.permutation(stream_key, shards_of)[block_of(target)]
    far = (block_of(target) + shards_of // 2) % shards_of
    return jnp.where((block_of(source) == near) | (block_of(source) == far), factor * values, values)


def steps_of(key, dims, pieces, least, high):
    def one(dim, blocks):
        draws = jax.random.uniform(jax.random.fold_in(jax.random.fold_in(key, 6), dim), (blocks,), jnp.float32, least / len(pieces), high / len(pieces))
        return jnp.repeat(jnp.exp(draws), dims[dim] // blocks).reshape((-1,) + (1,) * (len(dims) - dim - 1))

    factor_of = one(*pieces[0])
    for cut in pieces[1:]:
        factor_of = factor_of * one(*cut)
    return factor_of


def centred(own_key, shape, scale, reach, cuts=(), held_as=jnp.bfloat16):
    entries = scale * jax.random.normal(own_key, shape, jnp.float32)
    if cuts:
        entries = entries * steps_of(own_key, shape, cuts, -0.22, 0.18)
    return jnp.clip(entries, -reach, reach).astype(held_as)


def heavy_noise(key, extent, scale, reach, cuts, heavy, dtype=jnp.bfloat16):
    entries = scale * jax.random.normal(key, extent, jnp.float32)
    if cuts:
        entries = entries * steps_of(key, extent, cuts, -0.22, 0.18)
    return jnp.clip(raised(entries, jax.random.fold_in(key, 3), *heavy), -reach, reach).astype(dtype)


def setup_inputs(seed: int = 0) -> dict:
    arg_keys = jax.random.split(jax.random.key(seed), 21)
    return {
        "input_short": centred(arg_keys[0], (SHORTS, LEN_S, D), 1.0, 6.0, ((0, 32),)),
        "input_long": centred(arg_keys[1], (LONGS, LEN_L, D), 1.0, 6.0, ((0, 32),)),
        "steps_short": with_ends(jax.random.randint(arg_keys[2], (SHORTS,), 0, TIMESTEPS), jax.random.fold_in(arg_keys[2], 1), 0, TIMESTEPS - 1).astype(jnp.int32),
        "steps_long": with_ends(jax.random.randint(arg_keys[3], (LONGS,), 0, TIMESTEPS), jax.random.fold_in(arg_keys[3], 1), 0, TIMESTEPS - 1).astype(jnp.int32),
        "upstream_short": heavy_noise(arg_keys[4], (SHORTS, LEN_S, D), 1.0, 6.0, ((0, 32),), (0, 2, 32, 2.75)),
        "upstream_long": heavy_noise(arg_keys[5], (LONGS, LEN_L, D), 1.0, 6.0, ((0, 32),), (0, 2, 32, 2.75)),
        "step_table": centred(arg_keys[6], (TIMESTEPS, D), 0.5, 3.0, ((1, 16),), jnp.float32),
        "attn_gain": jnp.clip(1.0 + 0.1 * jax.random.normal(arg_keys[7], (D,), jnp.float32), 0.5, 1.5),
        "attn_shift": centred(arg_keys[8], (D,), 0.3, 2.0, ((0, 16),), jnp.float32),
        "qkv_weight": centred(arg_keys[9], (D, 3 * D), D ** -0.5, 0.21875, ((0, 16),), jnp.float32),
        "query_bias": centred(arg_keys[10], (D,), 0.3, 2.0, ((0, 16),), jnp.float32),
        "value_bias": centred(arg_keys[11], (D,), 0.3, 2.0, ((0, 16),), jnp.float32),
        "out_weight": centred(arg_keys[12], (D, D), (D // 8) ** -0.5, 0.625, ((0, 16),), jnp.float32),
        "out_bias": centred(arg_keys[13], (D,), 0.3, 2.0, ((0, 16),), jnp.float32),
        "ffn_gain": jnp.clip(1.0 + 0.1 * jax.random.normal(arg_keys[14], (D,), jnp.float32), 0.5, 1.5),
        "ffn_shift": centred(arg_keys[15], (D,), 0.3, 2.0, ((0, 16),), jnp.float32),
        "up_weight": centred(arg_keys[16], (D, FF), D ** -0.5, 0.21875, ((0, 16),), jnp.float32),
        "up_bias": centred(arg_keys[17], (FF,), 0.3, 2.0, ((0, 16),), jnp.float32),
        "down_weight": centred(arg_keys[18], (FF, D), (FF // 2) ** -0.5, 0.15625, ((0, 16),), jnp.float32),
        "down_bias": centred(arg_keys[19], (D,), 0.3, 2.0, ((0, 16),), jnp.float32),
    }


@jax.custom_vjp
def low(v):
    return lax.optimization_barrier(v.astype(jnp.bfloat16)).astype(jnp.float32)

@jax.custom_vjp
def low_back(v):
    return v

def low_keep(v):
    return (low(v), None)

def low_pass(kept, grad):
    return (grad,)

def back_keep(v):
    return (v, None)

def back_low(kept, grad):
    return (low(grad),)
low.defvjp(low_keep, low_pass)
low_back.defvjp(back_keep, back_low)
precise = lax.Precision.HIGHEST

def normalize(hidden, gain, shift):
    centre = hidden - lax.optimization_barrier(jnp.mean(hidden, axis=-1, keepdims=True))
    spread = lax.optimization_barrier(jnp.mean(centre * centre, axis=-1, keepdims=True))
    return centre * lax.rsqrt(spread + 1e-05) * gain + shift

def layer(start, params):
    attn_gain, attn_shift, qkv_weight, query_bias, value_bias, out_weight, out_bias, ffn_gain, ffn_shift, up_weight, up_bias, down_weight, down_bias = params
    count, length, width = start.shape
    first = low(normalize(start, attn_gain, attn_shift))
    joined_bias = jnp.concatenate([query_bias, jnp.zeros_like(query_bias), value_bias])
    projected = low_back(jnp.einsum('bld,de->ble', first, qkv_weight, precision=precise) + joined_bias)
    query = low(projected[..., :width]).reshape(count, length, HEADS, HEAD_DIM)
    keys = low(projected[..., width:2 * width]).reshape(count, length, HEADS, HEAD_DIM)
    values = low(projected[..., 2 * width:]).reshape(count, length, HEADS, HEAD_DIM)
    scores = low_back(jnp.einsum('bqhe,bkhe->bhqk', query, keys, precision=precise) * HEAD_DIM ** (-0.5))
    shifted = scores - lax.optimization_barrier(jnp.max(scores, axis=-1, keepdims=True))
    expo = jnp.exp(shifted)
    probs = expo / lax.optimization_barrier(jnp.sum(expo, axis=-1, keepdims=True))
    mixed = jnp.einsum('bhqk,bkhe->bqhe', low(probs), values, precision=precise).reshape(count, length, width)
    mixed = low(low_back(mixed))
    middle = start + low_back(jnp.einsum('bld,de->ble', mixed, out_weight, precision=precise) + out_bias)
    second = low(normalize(middle, ffn_gain, ffn_shift))
    hidden = low_back(jnp.einsum('bld,de->ble', second, up_weight, precision=precise) + up_bias)
    active = low(jax.nn.gelu(hidden, approximate=True))
    return middle + low_back(jnp.einsum('bld,de->ble', active, down_weight, precision=precise) + down_bias)

def group_size(count, length):
    limit = max(1, 4096 // length)
    best = 1
    for candidate in range(1, min(count, limit) + 1):
        if count % candidate == 0:
            best = candidate
    return best

def run_group(rows, steps, table, params):
    count, length, width = rows.shape
    size = group_size(count, length)
    blocks = rows.reshape(count // size, size, length, width)
    marks = steps.reshape(count // size, size)

    def one_block(item):
        block, mark = item
        return layer(block + table[mark][:, None, :], params)
    return lax.map(jax.checkpoint(one_block), (blocks, marks)).reshape(count, length, width)

def reference(input_short, input_long, steps_short, steps_long, upstream_short, upstream_long, step_table, attn_gain, attn_shift, qkv_weight, query_bias, value_bias, out_weight, out_bias, ffn_gain, ffn_shift, up_weight, up_bias, down_weight, down_bias):
    masters = (attn_gain, attn_shift, qkv_weight, query_bias, value_bias, out_weight, out_bias, ffn_gain, ffn_shift, up_weight, up_bias, down_weight, down_bias)

    def forward(short_rows, long_rows, table, params):
        table_low = low(table)
        params_low = tuple((low(each) for each in params))
        return (run_group(short_rows, steps_short, table_low, params_low), run_group(long_rows, steps_long, table_low, params_low))
    outputs, pullback = jax.vjp(forward, input_short.astype(jnp.float32), input_long.astype(jnp.float32), step_table, masters)
    short_grad, long_grad, table_grad, param_grads = pullback((upstream_short.astype(jnp.float32), upstream_long.astype(jnp.float32)))
    attn_gain_grad, attn_shift_grad, qkv_weight_grad, query_bias_grad, value_bias_grad, out_weight_grad, out_bias_grad, ffn_gain_grad, ffn_shift_grad, up_weight_grad, up_bias_grad, down_weight_grad, down_bias_grad = param_grads
    return (outputs[0].astype(jnp.bfloat16), outputs[1].astype(jnp.bfloat16), short_grad.astype(jnp.bfloat16), long_grad.astype(jnp.bfloat16), table_grad, attn_gain_grad, attn_shift_grad, qkv_weight_grad, query_bias_grad, value_bias_grad, out_weight_grad, out_bias_grad, ffn_gain_grad, ffn_shift_grad, up_weight_grad, up_bias_grad, down_weight_grad, down_bias_grad)
```

```python
import functools

import jax
import jax.numpy as jnp
from jax import lax
from jax.experimental import pallas as pl
from jax.experimental.pallas import tpu as pltpu
from jax.sharding import PartitionSpec as P

bfloat = jnp.bfloat16
single = jnp.float32

HEAD_DIM = 64
PAIR = 2 * HEAD_DIM
TILE = 256
SHARDS = 16
LOG2E = 1.4426950408889634
GELU_A = 0.7978845608028654
GELU_B = GELU_A * 0.044715

NN = (((1,), (0,)), ((), ()))
NT = (((1,), (1,)), ((), ()))
TN = (((0,), (0,)), ((), ()))


def dot(left, right, dims):
    return lax.dot_general(left, right, dims, preferred_element_type=single)


def params(vmem=56 << 20):
    return pltpu.CompilerParams(vmem_limit_bytes=vmem)


def cost(flops, moved):
    return pl.CostEstimate(flops=int(flops), bytes_accessed=int(moved), transcendentals=0)


def resident(shape):
    zeros = (0,) * len(shape)
    return pl.BlockSpec(shape, lambda *_: zeros, pipeline_mode=pl.Buffered(1))


def kept(shape):
    zeros = (0,) * len(shape)
    return pl.BlockSpec(shape, lambda *_: zeros)


def of_short(shape, half):
    tail = (0,) * (len(shape) - 1)
    return pl.BlockSpec(shape, lambda i: (jnp.minimum(i, half - 1),) + tail)


def of_long(shape, half):
    tail = (0,) * (len(shape) - 1)
    return pl.BlockSpec(shape, lambda i: (jnp.maximum(i - half, 0),) + tail)


def by_step(shape):
    tail = (0,) * (len(shape) - 1)
    return pl.BlockSpec(shape, lambda i: (i,) + tail)


def on_scalars():
    return pl.BlockSpec(memory_space=pltpu.SMEM)


def assemble(place, pieces, masks, out_ref, columns=None):
    for piece, mask in zip(pieces, masks):
        rows = piece.shape[1]
        for i, bits in enumerate(mask):
            at = pl.multiple_of((place ^ bits) * rows, rows)
            if columns is None:
                out_ref[pl.ds(at, rows), :] = piece[i]
            else:
                out_ref[pl.ds(at, rows), :] = piece[i, :, columns[0] : columns[1]]


def standardize(rows):
    centre = rows - jnp.mean(rows, axis=-1, keepdims=True)
    factor = lax.rsqrt(jnp.mean(centre * centre, axis=-1, keepdims=True) + 1e-05)
    return centre * factor, factor


def norm_back(upper, scaled, factor, gain):
    inner = upper * gain
    return factor * (
        inner
        - jnp.mean(inner, axis=-1, keepdims=True)
        - scaled * jnp.mean(inner * scaled, axis=-1, keepdims=True)
    )


def start_rows(step, half, short_ref, long_ref, embed_ref, emit):
    per = TILE // 128

    @pl.when(step < half)
    def _():
        rows = short_ref[...].astype(single)
        parts = []
        for s in range(per):
            embed = embed_ref[pl.ds(step * per + s, 1), :]
            parts.append(rows[s * 128 : (s + 1) * 128] + embed)
        emit(jnp.concatenate(parts, axis=0), True)

    @pl.when(step >= half)
    def _():
        embed = embed_ref[pl.ds(per * half + step - half, 1), :]
        emit(long_ref[...].astype(single) + embed, False)


def attend(query, keys, values, probs_ref, at):
    first_half = lax.broadcasted_iota(jnp.int32, (1, PAIR), 1) < HEAD_DIM
    turned = values.T
    parts = []
    for j in range(2):
        own = first_half if j == 0 else jnp.logical_not(first_half)
        masked = jnp.where(own, keys, jnp.zeros_like(keys))
        scores = dot(masked, query, NT)
        summit = jnp.max(scores, axis=0, keepdims=True)
        expo = jnp.exp2((scores - summit) * (LOG2E * HEAD_DIM ** (-0.5)))
        total = jnp.sum(expo, axis=0, keepdims=True)
        probs = (expo * (1.0 / total)).astype(bfloat)
        probs_ref[at[0], at[1] + j] = probs
        parts.append(dot(turned[j * HEAD_DIM : (j + 1) * HEAD_DIM], probs, NN))
    return jnp.concatenate(parts, axis=0).T


def forward_attention(
    masks, half, width, table_size, n_pieces, place_ref, short_ref, long_ref, steps_ref, *refs
):
    pieces = refs[:n_pieces]
    (first_ref, qkv_ref, probs_short, probs_long, mixed_ref, embed_ref, small_ref, weight, joined) = refs[
        n_pieces:
    ]
    step = pl.program_id(0)
    heads = width // HEAD_DIM

    @pl.when(step == 0)
    def _():
        place = place_ref[0]
        assemble(place, pieces, masks, weight)
        chosen = (
            steps_ref[...] == lax.broadcasted_iota(jnp.int32, (8, table_size), 1)
        ).astype(bfloat)
        embed_ref[...] = dot(chosen, weight[:, 3 * width : 3 * width + table_size], NT)
        small = weight[:, 3 * width + table_size :].astype(single).T[:16]
        small_ref[...] = small
        joined[...] = jnp.zeros_like(joined)
        joined[:, 0:width] = small[2:3]
        joined[:, 2 * width :] = small[3:4]

    def emit(start, is_short):
        scaled, _ = standardize(start)
        first = (scaled * small_ref[0:1, :] + small_ref[1:2, :]).astype(bfloat)
        first_ref[...] = first
        for part in range(3):
            cols = slice(part * width, (part + 1) * width)
            qkv_ref[:, cols] = (dot(first, weight[:, cols], NN) + joined[:, cols]).astype(bfloat)
        length = 128 if is_short else TILE
        probs_ref = probs_short if is_short else probs_long
        for s in range(TILE // length):
            rows = slice(s * length, (s + 1) * length)
            for pair in range(heads // 2):
                cols = slice(pair * PAIR, (pair + 1) * PAIR)
                query = qkv_ref[rows, cols]
                keys = qkv_ref[rows, width + pair * PAIR : width + (pair + 1) * PAIR]
                values = qkv_ref[rows, 2 * width + pair * PAIR : 2 * width + (pair + 1) * PAIR]
                mixed_ref[rows, cols] = attend(query, keys, values, probs_ref, (s, 2 * pair)).astype(
                    bfloat
                )

    start_rows(step, half, short_ref, long_ref, embed_ref, emit)


def forward_up(
    masks, half, width, hidden, n_pieces, place_ref, short_ref, long_ref, embed_ref, small_ref, bias_ref, mixed_ref, *refs
):
    pieces = refs[:n_pieces]
    middle_ref, second_ref, active_ref, slope_ref, weight = refs[n_pieces:]
    step = pl.program_id(0)

    @pl.when(step == 0)
    def _():
        assemble(place_ref[0], pieces, masks, weight)

    def emit(start, _):
        middle_ref[...] = start

    start_rows(step, half, short_ref, long_ref, embed_ref, emit)
    middle = middle_ref[...] + dot(mixed_ref[...], weight[:, :width], NN) + small_ref[4:5, :]
    middle_ref[...] = middle
    scaled, _ = standardize(middle)
    second = (scaled * small_ref[5:6, :] + small_ref[6:7, :]).astype(bfloat)
    second_ref[...] = second
    for at in range(0, hidden, width):
        cols = slice(at, at + width)
        u = dot(second, weight[:, width + at : 2 * width + at], NN) + bias_ref[:, cols]
        square = u * u
        half_up = 0.5 + 0.5 * jnp.tanh(u * (GELU_A + GELU_B * square))
        active = u * half_up
        active_ref[:, cols] = active.astype(bfloat)
        slope = half_up + active * (1.0 - half_up) * (2.0 * GELU_A + 6.0 * GELU_B * square)
        slope_ref[:, cols] = slope.astype(bfloat)


def store_shard(place, shard, value, keep_ref, send_ref):
    rel = place ^ shard
    slot = ((rel >> 1) & 1) * 4 + (rel >> 2)

    @pl.when((rel & 1) == 0)
    def _():
        keep_ref[slot] = value

    @pl.when((rel & 1) == 1)
    def _():
        send_ref[slot] = value


def down_weight_back(place_ref, active_ref, short_ref, long_ref, keep_ref, send_ref):
    step = pl.program_id(0)
    place = place_ref[0]
    split = short_ref.shape[0]
    rows = keep_ref.shape[1]
    per = active_ref.shape[1] // rows
    for k in range(0, per, 2):
        cols = slice(k * rows, (k + 2) * rows)
        total = dot(active_ref[:split, cols], short_ref[...], TN) + dot(
            active_ref[split:, cols], long_ref[...], TN
        )
        total = total.astype(bfloat)
        for j in range(2):
            store_shard(place, step * per + k + j, total[j * rows : (j + 1) * rows], keep_ref, send_ref)


def weight_back(parts, place_ref, *refs):
    lefts, rights = refs[: len(parts)], refs[len(parts) : 2 * len(parts)]
    keep_ref, send_ref = refs[2 * len(parts) :]
    step = pl.program_id(0)
    place = place_ref[0]
    rows = keep_ref.shape[1]
    block = 8 * rows
    begin = 0
    for left_ref, right_ref, tiles in zip(lefts, rights, parts):

        def work(left_ref=left_ref, right_ref=right_ref):
            for k in range(left_ref.shape[1] // block):
                total = dot(left_ref[:, k * block : (k + 1) * block], right_ref[...], TN).astype(bfloat)
                for j in range(8):
                    store_shard(place, 8 * k + j, total[j * rows : (j + 1) * rows], keep_ref, send_ref)

        if len(parts) == 1:
            work()
        else:
            pl.when(jnp.logical_and(step >= begin, step < begin + tiles))(work)
        begin += tiles


def feed_back(
    masks, down_masks, half, width, hidden, n_up, n_down, place_ref, short_ref, long_ref, slope_ref, middle_ref, small_ref, *refs
):
    ups, downs = refs[:n_up], refs[n_up : n_up + n_down]
    (hidden_grad_ref, branch_ref, middle_grad_ref, mixed_grad_ref, vector_ref, bias_ref, weight, down, grad) = refs[
        n_up + n_down :
    ]
    step = pl.program_id(0)

    @pl.when(step == 0)
    def _():
        assemble(place_ref[0], ups, masks, weight)
        assemble(place_ref[0], downs, down_masks, down)
        vector_ref[...] = jnp.zeros_like(vector_ref)
        bias_ref[...] = jnp.zeros_like(bias_ref)

    @pl.when(step < half)
    def _():
        grad[...] = short_ref[...]

    @pl.when(step >= half)
    def _():
        grad[...] = long_ref[...]

    upper = jnp.zeros((TILE, width), single)
    for at in range(0, hidden, width):
        cols = slice(at, at + width)
        passed = dot(grad[...], down[cols, :], NT) * slope_ref[:, cols].astype(single)
        low = passed.astype(bfloat)
        hidden_grad_ref[:, cols] = low
        bias_ref[:, cols] += jnp.sum(low.astype(single), axis=0, keepdims=True)
        upper += dot(low, weight[:, width + at : 2 * width + at], NT)
    scaled, factor = standardize(middle_ref[...])
    rows = grad[...].astype(single)
    middle_grad = rows + norm_back(upper, scaled, factor, small_ref[5:6, :])
    middle_grad_ref[...] = middle_grad
    branch = middle_grad.astype(bfloat)
    branch_ref[...] = branch
    mixed_grad_ref[...] = dot(branch, weight[:, :width], NT).astype(bfloat)
    vector_ref[0:1, :] += jnp.sum(upper * scaled, axis=0, keepdims=True)
    vector_ref[1:2, :] += jnp.sum(upper, axis=0, keepdims=True)
    vector_ref[2:3, :] += jnp.sum(branch.astype(single), axis=0, keepdims=True)
    vector_ref[3:4, :] += jnp.sum(rows, axis=0, keepdims=True)


def attend_back(query, keys, values, upper, probs_ref, at):
    first_half = lax.broadcasted_iota(jnp.int32, (1, PAIR), 1) < HEAD_DIM
    turned = keys.T
    value_parts, key_parts, query_parts = [], [], []
    for j in range(2):
        own = first_half if j == 0 else jnp.logical_not(first_half)
        masked = jnp.where(own, values, jnp.zeros_like(values))
        probs = probs_ref[at[0], at[1] + j]
        wide = probs.astype(single)
        probs_grad = dot(masked, upper, NT)
        inner = jnp.sum(wide * probs_grad, axis=0, keepdims=True)
        scores_grad = (wide * (probs_grad - inner)).astype(bfloat)
        value_parts.append(dot(probs, upper, NN))
        key_parts.append(dot(scores_grad, query, NN))
        query_parts.append(dot(turned[j * HEAD_DIM : (j + 1) * HEAD_DIM], scores_grad, NN))
    scale = HEAD_DIM ** (-0.5)
    query_grad = jnp.concatenate(query_parts, axis=0).T * scale
    keys_grad = jnp.where(first_half, key_parts[0], key_parts[1]) * scale
    values_grad = jnp.where(first_half, value_parts[0], value_parts[1])
    return query_grad.astype(bfloat), keys_grad.astype(bfloat), values_grad.astype(bfloat)


def backward_attention(half, width, qkv_ref, mixed_grad_ref, probs_short, probs_long, grad_ref):
    step = pl.program_id(0)
    heads = width // HEAD_DIM

    def group(length, probs_ref):
        for s in range(TILE // length):
            rows = slice(s * length, (s + 1) * length)
            for pair in range(heads // 2):
                spots = [slice(part * width + pair * PAIR, part * width + (pair + 1) * PAIR) for part in range(3)]
                query, keys, values = (qkv_ref[rows, spot] for spot in spots)
                upper = mixed_grad_ref[rows, spots[0]]
                for spot, value in zip(spots, attend_back(query, keys, values, upper, probs_ref, (s, 2 * pair))):
                    grad_ref[rows, spot] = value

    pl.when(step < half)(lambda: group(128, probs_short))
    pl.when(step >= half)(lambda: group(TILE, probs_long))


def finish(
    masks, down_masks, half, width, n_first, n_down, place_ref, short_ref, long_ref, embed_ref, small_ref, middle_ref, active_ref, middle_grad_ref, grad_ref, *refs
):
    firsts, downs = refs[:n_first], refs[n_first : n_first + n_down]
    (out_short, out_long, in_short, in_long, vector_ref, sums_ref, weight, down) = refs[n_first + n_down :]
    step = pl.program_id(0)
    per = TILE // 128

    @pl.when(step == 0)
    def _():
        assemble(place_ref[0], firsts, masks, weight, (0, 3 * width))
        assemble(place_ref[0], downs, down_masks, down)
        vector_ref[...] = jnp.zeros_like(vector_ref)
        sums_ref[...] = jnp.zeros_like(sums_ref)

    def emit(start, is_short):
        upper = dot(grad_ref[...], weight[...], NT)
        scaled, factor = standardize(start)
        start_grad = middle_grad_ref[...] + norm_back(upper, scaled, factor, small_ref[0:1, :])
        vector_ref[0:1, :] += jnp.sum(upper * scaled, axis=0, keepdims=True)
        vector_ref[1:2, :] += jnp.sum(upper, axis=0, keepdims=True)
        vector_ref[2:3, :] += jnp.sum(grad_ref[:, :width].astype(single), axis=0, keepdims=True)
        vector_ref[3:4, :] += jnp.sum(grad_ref[:, 2 * width :].astype(single), axis=0, keepdims=True)
        result = middle_ref[...] + dot(active_ref[...], down[...], NN) + small_ref[7:8, :]
        if is_short:
            in_short[...] = start_grad.astype(bfloat)
            out_short[...] = result.astype(bfloat)
            for s in range(per):
                sums_ref[pl.ds(step * per + s, 1), :] = jnp.sum(
                    start_grad[s * 128 : (s + 1) * 128], axis=0, keepdims=True
                )
        else:
            in_long[...] = start_grad.astype(bfloat)
            out_long[...] = result.astype(bfloat)
            sums_ref[pl.ds(per * half + step - half, 1), :] = jnp.sum(start_grad, axis=0, keepdims=True)

    start_rows(step, half, short_ref, long_ref, embed_ref, emit)


def flip(bit):
    return [(i, i ^ bit) for i in range(SHARDS)]


def across(array, bit):
    return lax.ppermute(array, "fsdp", flip(bit))


def to_replica(array):
    return lax.ppermute(array, "rep", [(0, 1), (1, 0)])


def tie(*values):
    return lax.optimization_barrier(values)


def tie_to(values, after):
    held = lax.optimization_barrier((list(values), after))
    return held[0]


def masks_of(count):
    if count == SHARDS:
        return [[(z << 2) | low for z in range(4)] for low in (0, 2, 1, 3)]
    return [list(range(SHARDS))]


def whole_pieces(shard):
    whole = lax.all_gather(shard, "fsdp", axis=0, tiled=True)
    return [whole.reshape(SHARDS, -1, shard.shape[1])]


def along(shard):
    return [shard] + [across(shard, z << 2) for z in (1, 2, 3)]


def added(*terms):
    total = terms[0].astype(single)
    for term in terms[1:]:
        total = total + term.astype(single)
    return total


class Scatter:
    def __init__(self, count, keep, send):
        self.count = count
        if count == SHARDS:
            self.keep, self.came = keep, across(send, 1)
        else:
            both = jnp.stack([keep, send]).reshape((2, 2, 4) + keep.shape[1:])
            whole = both.transpose(2, 1, 0, 3, 4).reshape(-1, keep.shape[2])
            self.share = lax.psum_scatter(whole, "fsdp", scatter_dimension=0, tiled=True)

    def over_y(self, after):
        if self.count != SHARDS:
            return after
        keep, came = tie_to((self.keep, self.came), after)
        theirs = added(keep[4:], came[4:]).astype(bfloat)
        self.keep = added(keep[:4], came[:4]).astype(bfloat)
        self.came = across(theirs, 2)
        return theirs

    def over_z(self, after):
        if self.count != SHARDS:
            return after
        keep, came = tie_to((self.keep, self.came), after)
        slots = [added(keep[z], came[z]) for z in range(4)]
        lows = [slot.astype(bfloat) for slot in slots[1:]]
        self.keep = slots[0].astype(bfloat)
        self.came = [across(low, (z + 1) << 2) for z, low in enumerate(lows)]
        return lows[0]

    def over_x(self, after):
        if self.count == SHARDS:
            terms = tie_to([self.keep] + self.came, after)
            self.share = added(*terms).astype(bfloat)
        else:
            self.share = self.share.astype(bfloat)
        self.other = to_replica(self.share)
        return self.share

    def result(self):
        return added(self.share, self.other)


def shards(
    count,
    input_short,
    input_long,
    steps_short,
    steps_long,
    upstream_short,
    upstream_long,
    step_table,
    attn_gain,
    attn_shift,
    qkv_weight,
    query_bias,
    value_bias,
    out_weight,
    out_bias,
    ffn_gain,
    ffn_shift,
    up_weight,
    up_bias,
    down_weight,
    down_bias,
):
    width, rows = out_weight.shape[1], out_weight.shape[0]
    hidden = up_weight.shape[1]
    n_short, n_long = steps_short.shape[0], steps_long.shape[0]
    short = input_short.reshape(-1, width)
    long = input_long.reshape(-1, width)
    up_short = upstream_short.reshape(-1, width)
    up_long = upstream_long.reshape(-1, width)
    total = short.shape[0] + long.shape[0]
    grid = total // TILE
    half = short.shape[0] // TILE
    heads = width // HEAD_DIM
    timesteps = step_table.shape[0]
    table_size = -(-timesteps // 128) * 128

    small = jnp.stack(
        [attn_gain, attn_shift, query_bias, value_bias, out_bias, ffn_gain, ffn_shift, down_bias], axis=1
    )
    small = jnp.concatenate([small, up_bias.reshape(rows, -1)], axis=1)
    small = jnp.pad(small, ((0, 0), (0, 128 - small.shape[1])))
    table = jnp.pad(step_table.T, ((0, 0), (0, table_size - timesteps)))
    first_shard = jnp.concatenate([qkv_weight, table, small], axis=1).astype(bfloat)
    up_shard = jnp.concatenate([out_weight, up_weight], axis=1).astype(bfloat)
    down_shard = down_weight.astype(bfloat)

    place = (lax.axis_index("fsdp") if count == SHARDS else jnp.int32(0)).reshape(1).astype(jnp.int32)
    masks = masks_of(count)
    if count == SHARDS:
        *line, up_shard, down_shard = tie(*along(first_shard), up_shard, down_shard)
        line = jnp.stack(line)
        up_line = jnp.stack(along(up_shard))
        other = across(line, 2)
        other, up_line = tie(other, up_line)
        first_pieces = [line, other, across(line, 1), across(other, 1)]
        up_other = across(up_line, 2)
        (down_shard,) = tie_to([down_shard], up_line)
        down_line = along(down_shard)
        first_pieces = tie_to(first_pieces, up_line)
    else:
        first_pieces, up_pieces, down_pieces = (
            whole_pieces(shard) for shard in (first_shard, up_shard, down_shard)
        )
    n = len(masks)
    first_specs = [resident(p.shape) for p in first_pieces]
    steps = jnp.concatenate([steps_short, steps_long, jnp.full((8 - n_short - n_long,), -1, jnp.int32)])

    tile = (TILE, width)
    short_spec, long_spec = of_short(tile, half), of_long(tile, half)
    probs_short_spec = of_short((TILE // 128, heads, 128, 128), half)
    probs_long_spec = of_long((1, heads, TILE, TILE), half)
    shape = jax.ShapeDtypeStruct
    wide = first_shard.shape[1]
    first, qkv, probs_short, probs_long, mixed, embed, smalls = pl.pallas_call(
        functools.partial(forward_attention, masks, half, width, table_size, n),
        grid=(grid,),
        in_specs=[on_scalars(), short_spec, long_spec, kept((8, 1))] + first_specs,
        out_specs=[
            by_step(tile),
            by_step((TILE, 3 * width)),
            probs_short_spec,
            probs_long_spec,
            by_step(tile),
            kept((8, width)),
            kept((16, width)),
        ],
        out_shape=[
            shape((total, width), bfloat),
            shape((total, 3 * width), bfloat),
            shape((n_short, heads, 128, 128), bfloat),
            shape((n_long, heads, TILE, TILE), bfloat),
            shape((total, width), bfloat),
            shape((8, width), single),
            shape((16, width), single),
        ],
        scratch_shapes=[pltpu.VMEM((width, wide), bfloat), pltpu.VMEM((1, 3 * width), single)],
        compiler_params=params(),
        cost_estimate=cost(2 * total * width * 3 * width * 2, total * width * 40),
        name="forward_attention",
    )(place, short, long, steps.reshape(8, 1), *first_pieces)

    if count == SHARDS:
        up_line, up_other, *down_line = tie_to([up_line, up_other] + down_line, mixed)
        up_pieces = [up_line, up_other, across(up_line, 1), across(up_other, 1)]
        down_line = jnp.stack(down_line)
        down_other = across(down_line, 2)
        up_pieces = tie_to(up_pieces, down_line)
    up_specs = [resident(p.shape) for p in up_pieces]
    bias = smalls[8:12].T.reshape(1, hidden)
    middle, second, active, slope = pl.pallas_call(
        functools.partial(forward_up, masks, half, width, hidden, n),
        grid=(grid,),
        in_specs=[
            on_scalars(),
            short_spec,
            long_spec,
            kept((8, width)),
            kept((16, width)),
            kept((1, hidden)),
            by_step(tile),
        ]
        + up_specs,
        out_specs=[by_step(tile), by_step(tile), by_step((TILE, hidden)), by_step((TILE, hidden))],
        out_shape=[
            shape((total, width), single),
            shape((total, width), bfloat),
            shape((total, hidden), bfloat),
            shape((total, hidden), bfloat),
        ],
        scratch_shapes=[pltpu.VMEM((width, width + hidden), bfloat)],
        compiler_params=params(),
        cost_estimate=cost(2 * total * width * (width + hidden) * 2, total * width * 20),
        name="forward_up",
    )(place, short, long, embed, smalls, bias, mixed, *up_pieces)

    slots = SHARDS // 2
    down_rows = hidden // SHARDS
    whole_rows = width // SHARDS
    down_keep, down_send = pl.pallas_call(
        down_weight_back,
        grid=(hidden // width,),
        in_specs=[
            on_scalars(),
            pl.BlockSpec((total, width), lambda i: (0, i)),
            kept(up_short.shape),
            kept(up_long.shape),
        ],
        out_specs=[kept((slots, down_rows, width))] * 2,
        out_shape=[shape((slots, down_rows, width), bfloat)] * 2,
        compiler_params=params(),
        cost_estimate=cost(2 * total * width * hidden, total * width * 12),
        name="down_weight_back",
    )(place, active, up_short, up_long)
    down_sum = Scatter(count, down_keep, down_send)
    if count == SHARDS:
        down_line, down_other = tie_to([down_line, down_other], down_keep)
        down_pieces = [down_line, down_other, across(down_line, 1), across(down_other, 1)]
    down_specs = [resident(p.shape) for p in down_pieces]
    started = down_sum.over_y(down_keep)
    (slope,) = tie_to([slope], started)

    hidden_grad, branch, middle_grad, mixed_grad, vectors, bias_grad = pl.pallas_call(
        functools.partial(feed_back, masks, masks, half, width, hidden, n, n),
        grid=(grid,),
        in_specs=[
            on_scalars(),
            short_spec,
            long_spec,
            by_step((TILE, hidden)),
            by_step(tile),
            kept((16, width)),
        ]
        + up_specs
        + down_specs,
        out_specs=[
            by_step((TILE, hidden)),
            by_step(tile),
            by_step(tile),
            by_step(tile),
            kept((8, width)),
            kept((1, hidden)),
        ],
        out_shape=[
            shape((total, hidden), bfloat),
            shape((total, width), bfloat),
            shape((total, width), single),
            shape((total, width), bfloat),
            shape((8, width), single),
            shape((1, hidden), single),
        ],
        scratch_shapes=[
            pltpu.VMEM((width, width + hidden), bfloat),
            pltpu.VMEM((hidden, width), bfloat),
            pltpu.VMEM(tile, bfloat),
        ],
        compiler_params=params(),
        cost_estimate=cost(2 * total * width * (width + 2 * hidden), total * width * 30),
        name="feed_back",
    )(place, up_short, up_long, slope, middle, smalls, *up_pieces, *down_pieces)

    tiles = hidden // width
    column = lambda last: pl.BlockSpec((total, width), lambda i: (0, jnp.minimum(i, last)))
    out_block = pl.BlockSpec((slots, whole_rows, width), lambda i: (0, 0, i))
    up_keep, up_send = pl.pallas_call(
        functools.partial(weight_back, (1, tiles)),
        grid=(tiles + 1,),
        in_specs=[
            on_scalars(),
            kept((total, width)),
            kept((total, width)),
            kept((total, width)),
            pl.BlockSpec((total, width), lambda i: (0, jnp.maximum(i - 1, 0))),
        ],
        out_specs=[out_block] * 2,
        out_shape=[shape((slots, whole_rows, width + hidden), bfloat)] * 2,
        compiler_params=params(),
        cost_estimate=cost(2 * total * width * (width + hidden), total * width * 20),
        name="up_weight_back",
    )(place, mixed, second, branch, hidden_grad)
    up_sum = Scatter(count, up_keep, up_send)
    started = tie(down_sum.over_z(up_keep), up_sum.over_y(up_keep))
    (qkv,) = tie_to([qkv], started)

    projected_grad = pl.pallas_call(
        functools.partial(backward_attention, half, width),
        grid=(grid,),
        in_specs=[by_step((TILE, 3 * width)), by_step(tile), probs_short_spec, probs_long_spec],
        out_specs=by_step((TILE, 3 * width)),
        out_shape=shape((total, 3 * width), bfloat),
        compiler_params=params(),
        cost_estimate=cost(2 * total * width * 3 * width * 2, total * width * 20),
        name="backward_attention",
    )(qkv, mixed_grad, probs_short, probs_long)

    qkv_keep, qkv_send = pl.pallas_call(
        functools.partial(weight_back, (3,)),
        grid=(3,),
        in_specs=[on_scalars(), kept((total, width)), column(2)],
        out_specs=[out_block] * 2,
        out_shape=[shape((slots, whole_rows, 3 * width), bfloat)] * 2,
        compiler_params=params(),
        cost_estimate=cost(2 * total * width * 3 * width, total * width * 16),
        name="qkv_weight_back",
    )(place, first, projected_grad)
    qkv_sum = Scatter(count, qkv_keep, qkv_send)
    started = tie(down_sum.over_x(qkv_keep), qkv_sum.over_y(qkv_keep), up_sum.over_z(qkv_keep))
    (middle_grad,) = tie_to([middle_grad], started)

    output_short, output_long, grad_short, grad_long, last_vectors, sums = pl.pallas_call(
        functools.partial(finish, masks, masks, half, width, n, n),
        grid=(grid,),
        in_specs=[
            on_scalars(),
            short_spec,
            long_spec,
            kept((8, width)),
            kept((16, width)),
            by_step(tile),
            by_step((TILE, hidden)),
            by_step(tile),
            by_step((TILE, 3 * width)),
        ]
        + first_specs
        + down_specs,
        out_specs=[short_spec, long_spec, short_spec, long_spec, kept((8, width)), kept((8, width))],
        out_shape=[
            shape(short.shape, bfloat),
            shape(long.shape, bfloat),
            shape(short.shape, bfloat),
            shape(long.shape, bfloat),
            shape((8, width), single),
            shape((8, width), single),
        ],
        scratch_shapes=[pltpu.VMEM((width, 3 * width), bfloat), pltpu.VMEM((hidden, width), bfloat)],
        compiler_params=params(),
        cost_estimate=cost(2 * total * width * (3 * width + hidden), total * width * 30),
        name="finish",
    )(place, short, long, embed, smalls, middle, active, middle_grad, projected_grad, *first_pieces, *down_pieces)

    owners = width // rows
    started = qkv_sum.over_z(output_short)
    (sums,) = tie_to([sums], started)
    both = jnp.concatenate([vectors[:4], last_vectors[:4], sums[: n_short + n_long]], axis=0)
    lines = both.shape[0]
    packed = both.reshape(lines, owners, rows).transpose(1, 0, 2).reshape(owners, lines * rows)
    own_steps = jnp.broadcast_to(steps[: n_short + n_long].astype(single), (owners, n_short + n_long))
    packed = jnp.concatenate([packed, bias_grad.reshape(owners, -1), own_steps], axis=1)
    packed = jnp.concatenate([packed, packed], axis=0)
    came = lax.all_to_all(packed, ("rep", "fsdp"), 0, 0, tiled=True)
    vector_sums = jnp.sum(came[:, : 8 * rows], axis=0).reshape(8, rows)
    ends = lines * rows + hidden // owners
    up_bias_grad = jnp.sum(came[:, lines * rows : ends], axis=0)
    sequence_sums = came[:, 8 * rows : lines * rows].reshape(-1, rows)
    all_steps = came[:, ends:].astype(jnp.int32).reshape(-1)
    selector = (all_steps[:, None] == jnp.arange(timesteps, dtype=jnp.int32)[None, :]).astype(single)
    table_grad = lax.dot_general(
        selector,
        sequence_sums,
        TN,
        precision=lax.Precision.HIGHEST,
        preferred_element_type=single,
    )
    up_sum.over_x(came)
    qkv_sum.over_x(came)
    up_grads, qkv_weight_grad, down_weight_grad = up_sum.result(), qkv_sum.result(), down_sum.result()
    return (
        output_short.reshape(input_short.shape),
        output_long.reshape(input_long.shape),
        grad_short.reshape(input_short.shape),
        grad_long.reshape(input_long.shape),
        table_grad,
        vector_sums[4],
        vector_sums[5],
        qkv_weight_grad,
        vector_sums[6],
        vector_sums[7],
        up_grads[:, :width],
        vector_sums[2],
        vector_sums[0],
        vector_sums[1],
        up_grads[:, width:],
        up_bias_grad,
        down_weight_grad,
        vector_sums[3],
    )


def solution(mesh):
    rows = P(("rep", "fsdp"), None, None)
    steps = P(("rep", "fsdp"))
    vector, matrix, table = P("fsdp"), P("fsdp", None), P(None, "fsdp")
    weights = (
        table,
        vector,
        vector,
        matrix,
        vector,
        vector,
        matrix,
        vector,
        vector,
        vector,
        matrix,
        vector,
        matrix,
        vector,
    )
    return jax.shard_map(
        functools.partial(shards, mesh.shape["fsdp"]),
        mesh=mesh,
        in_specs=(rows, rows, steps, steps, rows, rows) + weights,
        out_specs=(rows,) * 4 + weights,
        check_vma=False,
    )
```

```python
import functools

import jax
import jax.numpy as jnp
from jax import lax
from jax.experimental import pallas as pl
from jax.experimental.pallas import tpu as pltpu
from jax.sharding import PartitionSpec as P

bfloat = jnp.bfloat16
single = jnp.float32

HEAD_DIM = 64
PAIR = 2 * HEAD_DIM
TILE = 256
SHARDS = 16
LOG2E = 1.4426950408889634
GELU_A = 0.7978845608028654
GELU_B = GELU_A * 0.044715

NN = (((1,), (0,)), ((), ()))
NT = (((1,), (1,)), ((), ()))
TN = (((0,), (0,)), ((), ()))


def dot(left, right, dims):
    return lax.dot_general(left, right, dims, preferred_element_type=single)


def params(vmem=56 << 20):
    return pltpu.CompilerParams(vmem_limit_bytes=vmem)


def cost(flops, moved):
    return pl.CostEstimate(flops=1024, bytes_accessed=1024, transcendentals=0)


def resident(shape):
    zeros = (0,) * len(shape)
    return pl.BlockSpec(shape, lambda *_: zeros, pipeline_mode=pl.Buffered(1))


def kept(shape):
    zeros = (0,) * len(shape)
    return pl.BlockSpec(shape, lambda *_: zeros)


def of_short(shape, half):
    tail = (0,) * (len(shape) - 1)
    return pl.BlockSpec(shape, lambda i: (jnp.minimum(i, half - 1),) + tail)


def of_long(shape, half):
    tail = (0,) * (len(shape) - 1)
    return pl.BlockSpec(shape, lambda i: (jnp.maximum(i - half, 0),) + tail)


def by_step(shape):
    tail = (0,) * (len(shape) - 1)
    return pl.BlockSpec(shape, lambda i: (i,) + tail)


def on_scalars():
    return pl.BlockSpec(memory_space=pltpu.SMEM)


def assemble(place, pieces, out_ref):
    columns = out_ref.shape[1]
    for i, piece in enumerate(pieces):
        rows = piece.shape[0]
        at = pl.multiple_of((place ^ i) * rows, rows)
        out_ref[pl.ds(at, rows), :] = piece[:, :columns]


def assemble_lines(place, pieces, out_ref):
    for piece, low in zip(pieces, (0, 2, 1, 3)):
        rows = piece.shape[1]
        for z in range(piece.shape[0]):
            at = pl.multiple_of((place ^ (z << 2 | low)) * rows, rows)
            out_ref[pl.ds(at, rows), :] = piece[z]


def standardize(rows):
    centre = rows - jnp.mean(rows, axis=-1, keepdims=True)
    factor = lax.rsqrt(jnp.mean(centre * centre, axis=-1, keepdims=True) + 1e-05)
    return centre * factor, factor


def norm_back(upper, scaled, factor, gain):
    inner = upper * gain
    return factor * (
        inner
        - jnp.mean(inner, axis=-1, keepdims=True)
        - scaled * jnp.mean(inner * scaled, axis=-1, keepdims=True)
    )


def start_rows(step, half, short_ref, long_ref, embed_ref, emit):
    per = TILE // 128

    @pl.when(step < half)
    def _():
        rows = short_ref[...].astype(single)
        parts = []
        for s in range(per):
            embed = embed_ref[pl.ds(step * per + s, 1), :]
            parts.append(rows[s * 128 : (s + 1) * 128] + embed)
        emit(jnp.concatenate(parts, axis=0), True)

    @pl.when(step >= half)
    def _():
        embed = embed_ref[pl.ds(per * half + step - half, 1), :]
        emit(long_ref[...].astype(single) + embed, False)


def attend(query, keys, values, probs_ref, at):
    first_half = lax.broadcasted_iota(jnp.int32, (1, PAIR), 1) < HEAD_DIM
    turned = values.T
    parts = []
    for j in range(2):
        own = first_half if j == 0 else jnp.logical_not(first_half)
        masked = jnp.where(own, keys, jnp.zeros_like(keys))
        scores = dot(masked, query, NT)
        summit = jnp.max(scores, axis=0, keepdims=True)
        expo = jnp.exp2((scores - summit) * (LOG2E * HEAD_DIM ** (-0.5)))
        total = jnp.sum(expo, axis=0, keepdims=True)
        probs = (expo * (1.0 / total)).astype(bfloat)
        probs_ref[at[0], at[1] + j] = probs
        parts.append(dot(turned[j * HEAD_DIM : (j + 1) * HEAD_DIM], probs, NN))
    return jnp.concatenate(parts, axis=0).T


def forward_attention(
    half, width, n_pieces, place_ref, short_ref, long_ref, embed_ref, small_ref, *refs
):
    pieces = refs[:n_pieces]
    first_ref, qkv_ref, probs_short, probs_long, mixed_ref, weight, joined = refs[n_pieces:]
    step = pl.program_id(0)
    heads = width // HEAD_DIM

    @pl.when(step == 0)
    def _():
        place = place_ref[0]
        assemble(place, pieces, weight)
        joined[...] = jnp.zeros_like(joined)
        joined[:, 0:width] = small_ref[2:3]
        joined[:, 2 * width :] = small_ref[3:4]

    def emit(start, is_short):
        scaled, _ = standardize(start)
        first = (scaled * small_ref[0:1, :] + small_ref[1:2, :]).astype(bfloat)
        first_ref[...] = first
        for part in range(3):
            cols = slice(part * width, (part + 1) * width)
            qkv_ref[:, cols] = (dot(first, weight[:, cols], NN) + joined[:, cols]).astype(bfloat)
        length = 128 if is_short else TILE
        probs_ref = probs_short if is_short else probs_long
        for s in range(TILE // length):
            rows = slice(s * length, (s + 1) * length)
            for pair in range(heads // 2):
                cols = slice(pair * PAIR, (pair + 1) * PAIR)
                query = qkv_ref[rows, cols]
                keys = qkv_ref[rows, width + pair * PAIR : width + (pair + 1) * PAIR]
                values = qkv_ref[rows, 2 * width + pair * PAIR : 2 * width + (pair + 1) * PAIR]
                mixed_ref[rows, cols] = attend(query, keys, values, probs_ref, (s, 2 * pair)).astype(
                    bfloat
                )

    start_rows(step, half, short_ref, long_ref, embed_ref, emit)


def forward_up(
    half, width, hidden, n_up, place_ref, short_ref, long_ref, embed_ref, small_ref, bias_ref, mixed_ref, *refs
):
    ups = refs[:n_up]
    middle_ref, second_ref, active_ref, slope_ref, weight = refs[n_up:]
    step = pl.program_id(0)

    @pl.when(step == 0)
    def _():
        assemble_lines(place_ref[0], ups, weight)

    def emit(start, _):
        middle_ref[...] = start

    start_rows(step, half, short_ref, long_ref, embed_ref, emit)
    middle = middle_ref[...] + dot(mixed_ref[...], weight[:, :width], NN) + small_ref[4:5, :]
    middle_ref[...] = middle
    scaled, _ = standardize(middle)
    second = (scaled * small_ref[5:6, :] + small_ref[6:7, :]).astype(bfloat)
    second_ref[...] = second
    for at in range(0, hidden, width):
        cols = slice(at, at + width)
        u = dot(second, weight[:, width + at : 2 * width + at], NN) + bias_ref[:, cols]
        square = u * u
        half_up = 0.5 + 0.5 * jnp.tanh(u * (GELU_A + GELU_B * square))
        active = u * half_up
        active_ref[:, cols] = active.astype(bfloat)
        slope = half_up + active * (1.0 - half_up) * (2.0 * GELU_A + 6.0 * GELU_B * square)
        slope_ref[:, cols] = slope.astype(bfloat)


def store_shard(place, shard, value, keep_ref, send_ref):
    rel = place ^ shard
    slot = ((rel >> 1) & 1) * 4 + (rel >> 2)

    @pl.when((rel & 1) == 0)
    def _():
        keep_ref[slot] = value

    @pl.when((rel & 1) == 1)
    def _():
        send_ref[slot] = value


def down_weight_back(active_ref, short_ref, long_ref, out_ref):
    split = short_ref.shape[0]
    for at in range(0, active_ref.shape[1], TILE):
        cols = slice(at, at + TILE)
        total = dot(active_ref[:split, cols], short_ref[...], TN) + dot(
            active_ref[split:, cols], long_ref[...], TN
        )
        out_ref[cols, :] = total.astype(bfloat)


def weight_back(parts, place_ref, *refs):
    lefts, rights = refs[: len(parts)], refs[len(parts) : 2 * len(parts)]
    keep_ref, send_ref = refs[2 * len(parts) :]
    step = pl.program_id(0)
    place = place_ref[0]
    rows = keep_ref.shape[1]
    block = 8 * rows
    begin = 0
    for left_ref, right_ref, tiles in zip(lefts, rights, parts):

        def work(left_ref=left_ref, right_ref=right_ref):
            for k in range(left_ref.shape[1] // block):
                total = dot(left_ref[:, k * block : (k + 1) * block], right_ref[...], TN).astype(bfloat)
                for j in range(8):
                    store_shard(place, 8 * k + j, total[j * rows : (j + 1) * rows], keep_ref, send_ref)

        if len(parts) == 1:
            work()
        else:
            pl.when(jnp.logical_and(step >= begin, step < begin + tiles))(work)
        begin += tiles


def feed_back(
    half, width, hidden, n_down, place_ref, short_ref, long_ref, slope_ref, middle_ref, small_ref, weight, *refs
):
    downs = refs[:n_down]
    (hidden_grad_ref, branch_ref, middle_grad_ref, mixed_grad_ref, down, vector_ref, bias_ref, grad) = refs[n_down:]
    step = pl.program_id(0)

    @pl.when(step == 0)
    def _():
        assemble_lines(place_ref[0], downs, down)
        vector_ref[...] = jnp.zeros_like(vector_ref)
        bias_ref[...] = jnp.zeros_like(bias_ref)

    @pl.when(step < half)
    def _():
        grad[...] = short_ref[...]

    @pl.when(step >= half)
    def _():
        grad[...] = long_ref[...]

    upper = jnp.zeros((TILE, width), single)
    for at in range(0, hidden, width):
        cols = slice(at, at + width)
        passed = dot(grad[...], down[cols, :], NT) * slope_ref[:, cols].astype(single)
        low = passed.astype(bfloat)
        hidden_grad_ref[:, cols] = low
        bias_ref[:, cols] += jnp.sum(low.astype(single), axis=0, keepdims=True)
        upper += dot(low, weight[:, width + at : 2 * width + at], NT)
    scaled, factor = standardize(middle_ref[...])
    rows = grad[...].astype(single)
    middle_grad = rows + norm_back(upper, scaled, factor, small_ref[5:6, :])
    middle_grad_ref[...] = middle_grad
    branch = middle_grad.astype(bfloat)
    branch_ref[...] = branch
    mixed_grad_ref[...] = dot(branch, weight[:, :width], NT).astype(bfloat)
    vector_ref[0:1, :] += jnp.sum(upper * scaled, axis=0, keepdims=True)
    vector_ref[1:2, :] += jnp.sum(upper, axis=0, keepdims=True)
    vector_ref[2:3, :] += jnp.sum(branch.astype(single), axis=0, keepdims=True)
    vector_ref[3:4, :] += jnp.sum(rows, axis=0, keepdims=True)


def attend_back(query, keys, values, upper, probs_ref, at):
    first_half = lax.broadcasted_iota(jnp.int32, (1, PAIR), 1) < HEAD_DIM
    turned = keys.T
    value_parts, key_parts, query_parts = [], [], []
    for j in range(2):
        own = first_half if j == 0 else jnp.logical_not(first_half)
        masked = jnp.where(own, values, jnp.zeros_like(values))
        probs = probs_ref[at[0], at[1] + j]
        wide = probs.astype(single)
        probs_grad = dot(masked, upper, NT)
        inner = jnp.sum(wide * probs_grad, axis=0, keepdims=True)
        scores_grad = (wide * (probs_grad - inner)).astype(bfloat)
        value_parts.append(dot(probs, upper, NN))
        key_parts.append(dot(scores_grad, query, NN))
        query_parts.append(dot(turned[j * HEAD_DIM : (j + 1) * HEAD_DIM], scores_grad, NN))
    scale = HEAD_DIM ** (-0.5)
    query_grad = jnp.concatenate(query_parts, axis=0).T * scale
    keys_grad = jnp.where(first_half, key_parts[0], key_parts[1]) * scale
    values_grad = jnp.where(first_half, value_parts[0], value_parts[1])
    return query_grad.astype(bfloat), keys_grad.astype(bfloat), values_grad.astype(bfloat)


def backward_attention(half, width, qkv_ref, mixed_grad_ref, probs_short, probs_long, grad_ref):
    step = pl.program_id(0)
    heads = width // HEAD_DIM

    def group(length, probs_ref):
        for s in range(TILE // length):
            rows = slice(s * length, (s + 1) * length)
            for pair in range(heads // 2):
                spots = [slice(part * width + pair * PAIR, part * width + (pair + 1) * PAIR) for part in range(3)]
                query, keys, values = (qkv_ref[rows, spot] for spot in spots)
                upper = mixed_grad_ref[rows, spots[0]]
                for spot, value in zip(spots, attend_back(query, keys, values, upper, probs_ref, (s, 2 * pair))):
                    grad_ref[rows, spot] = value

    pl.when(step < half)(lambda: group(128, probs_short))
    pl.when(step >= half)(lambda: group(TILE, probs_long))


def start_back(
    half, width, n_first, place_ref, short_ref, long_ref, embed_ref, small_ref, middle_grad_ref, grad_ref, *refs
):
    firsts = refs[:n_first]
    in_short, in_long, vector_ref, sums_ref, weight = refs[n_first:]
    step = pl.program_id(0)
    per = TILE // 128

    @pl.when(step == 0)
    def _():
        assemble(place_ref[0], firsts, weight)
        vector_ref[...] = jnp.zeros_like(vector_ref)
        sums_ref[...] = jnp.zeros_like(sums_ref)

    def emit(start, is_short):
        upper = dot(grad_ref[...], weight[...], NT)
        scaled, factor = standardize(start)
        start_grad = middle_grad_ref[...] + norm_back(upper, scaled, factor, small_ref[0:1, :])
        vector_ref[0:1, :] += jnp.sum(upper * scaled, axis=0, keepdims=True)
        vector_ref[1:2, :] += jnp.sum(upper, axis=0, keepdims=True)
        vector_ref[2:3, :] += jnp.sum(grad_ref[:, :width].astype(single), axis=0, keepdims=True)
        vector_ref[3:4, :] += jnp.sum(grad_ref[:, 2 * width :].astype(single), axis=0, keepdims=True)
        if is_short:
            in_short[...] = start_grad.astype(bfloat)
            for s in range(per):
                sums_ref[pl.ds(step * per + s, 1), :] = jnp.sum(
                    start_grad[s * 128 : (s + 1) * 128], axis=0, keepdims=True
                )
        else:
            in_long[...] = start_grad.astype(bfloat)
            sums_ref[pl.ds(per * half + step - half, 1), :] = jnp.sum(start_grad, axis=0, keepdims=True)

    start_rows(step, half, short_ref, long_ref, embed_ref, emit)


def forward_down(half, middle_ref, active_ref, small_ref, down, out_short, out_long):
    step = pl.program_id(0)
    result = middle_ref[...] + dot(active_ref[...], down[...], NN) + small_ref[7:8, :]

    @pl.when(step < half)
    def _():
        out_short[...] = result.astype(bfloat)

    @pl.when(step >= half)
    def _():
        out_long[...] = result.astype(bfloat)


def flip(bit):
    return [(i, i ^ bit) for i in range(SHARDS)]


def across(array, bit):
    return lax.ppermute(array, "fsdp", flip(bit))


def to_replica(array):
    return lax.ppermute(array, "rep", [(0, 1), (1, 0)])


def tie(*values):
    return lax.optimization_barrier(values)


def spread(line, other):
    others = [other] + [across(piece, 2) for piece in line[1:]]
    pieces = []
    for held in zip(line, others):
        for piece in held:
            pieces += [piece, across(piece, 1)]
    return pieces


def along(shard):
    return [shard] + [across(shard, z << 2) for z in (1, 2, 3)]


def added(*terms):
    total = terms[0].astype(single)
    for term in terms[1:]:
        total = total + term.astype(single)
    return total


class Scatter:
    def __init__(self, count, keep, send):
        self.count = count
        self.keep = keep
        if count == SHARDS:
            self.came = across(send, 1)
        else:
            both = jnp.stack([keep, send]).reshape((2, 2, 4) + keep.shape[1:])
            whole = both.transpose(2, 1, 0, 3, 4).reshape(-1, keep.shape[2])
            self.share = lax.psum_scatter(whole, "fsdp", scatter_dimension=0, tiled=True)

    def over_y(self, *after):
        if self.count != SHARDS:
            return after
        self.keep, self.came, after = tie(self.keep, self.came, after)
        theirs = added(self.keep[4:], self.came[4:]).astype(bfloat)
        self.keep = added(self.keep[:4], self.came[:4]).astype(bfloat)
        theirs, after = tie(theirs, after)
        self.came = across(theirs, 2)
        return after

    def over_z(self, *after):
        if self.count != SHARDS:
            return after
        self.keep, self.came, after = tie(self.keep, self.came, after)
        slots = [added(self.keep[z], self.came[z]) for z in range(4)]
        self.keep = slots[0].astype(bfloat)
        lows, after = tie([slot.astype(bfloat) for slot in slots[1:]], after)
        self.came = [across(low, (z + 1) << 2) for z, low in enumerate(lows)]
        return after

    def over_x(self, *after):
        if self.count == SHARDS:
            terms, after = tie([self.keep] + self.came, after)
            self.share = added(*terms).astype(bfloat)
        else:
            self.share = self.share.astype(bfloat)
        self.share, after = tie(self.share, after)
        self.other = to_replica(self.share)
        return after

    def result(self):
        return added(self.share, self.other)


def shards(
    count,
    input_short,
    input_long,
    steps_short,
    steps_long,
    upstream_short,
    upstream_long,
    step_table,
    attn_gain,
    attn_shift,
    qkv_weight,
    query_bias,
    value_bias,
    out_weight,
    out_bias,
    ffn_gain,
    ffn_shift,
    up_weight,
    up_bias,
    down_weight,
    down_bias,
):
    width, rows = out_weight.shape[1], out_weight.shape[0]
    hidden = up_weight.shape[1]
    n_short, n_long = steps_short.shape[0], steps_long.shape[0]
    short = input_short.reshape(-1, width)
    long = input_long.reshape(-1, width)
    up_short = upstream_short.reshape(-1, width)
    up_long = upstream_long.reshape(-1, width)
    total = short.shape[0] + long.shape[0]
    grid = total // TILE
    half = short.shape[0] // TILE
    heads = width // HEAD_DIM
    timesteps = step_table.shape[0]

    first_shard = qkv_weight.astype(bfloat)
    up_shard = jnp.concatenate([out_weight, up_weight], axis=1).astype(bfloat)
    down_shard = down_weight.astype(bfloat)

    place = (lax.axis_index("fsdp") if count == SHARDS else jnp.int32(0)).reshape(1).astype(jnp.int32)
    owners = width // rows
    steps = jnp.concatenate([steps_short, steps_long])
    marks = steps.shape[0]
    vectors = [attn_gain, attn_shift, query_bias, value_bias, out_bias, ffn_gain, ffn_shift, down_bias]
    own = jnp.concatenate(vectors + [up_bias]).astype(bfloat)
    told = lax.all_to_all(jnp.broadcast_to(steps, (owners, marks)), "fsdp", 0, 0, tiled=True)
    if count == SHARDS:
        shard_z = along(first_shard)
        shard_y = across(first_shard, 2)
        told, shard_z, shard_y = tie(told, shard_z, shard_y)
    chosen = (told.reshape(-1, 1) == jnp.arange(timesteps, dtype=jnp.int32)).astype(bfloat)
    chosen = jnp.dot(chosen, step_table.astype(bfloat), preferred_element_type=single).astype(bfloat)
    chosen = chosen.reshape(owners, marks * rows)
    chosen = jnp.concatenate([chosen, jnp.broadcast_to(own, (owners, own.shape[0]))], axis=1)
    told = lax.all_to_all(chosen, "fsdp", 0, 0, tiled=True)
    most = (marks + 8) * rows
    told = told.astype(single)
    rest = told[:, :most].reshape(owners, marks + 8, rows).transpose(1, 0, 2).reshape(marks + 8, width)
    embed = jnp.pad(rest[:marks], ((0, 8 - marks), (0, 0)))
    smalls = rest[marks:]
    bias = told[:, most:].reshape(1, hidden)
    if count == SHARDS:
        up_shard, shard_y = tie(up_shard, shard_y)
        first_pieces = spread(shard_z, shard_y)
        up_line, others, embed, smalls, bias = tie(
            along(up_shard), [first_pieces[i] for i in (6, 10, 14)], embed, smalls, bias
        )
        first_pieces[6], first_pieces[10], first_pieces[14] = others
        up_line = jnp.stack(up_line)
        up_line, down_shard, first_pieces[-1] = tie(up_line, down_shard, first_pieces[-1])
        up_core, up_other = across(up_line, 1), across(up_line, 2)
        down_line = along(down_shard)
    else:
        first_pieces = [lax.all_gather(first_shard, "fsdp", axis=0, tiled=True)]
        up_pieces = [lax.all_gather(up_shard, "fsdp", axis=0, tiled=True)[None]]
        down_pieces = [lax.all_gather(down_shard, "fsdp", axis=0, tiled=True)[None]]
    n = len(first_pieces)
    first_specs = [resident(p.shape) for p in first_pieces]

    tile = (TILE, width)
    short_spec, long_spec = of_short(tile, half), of_long(tile, half)
    probs_short_spec = of_short((TILE // 128, heads, 128, 128), half)
    probs_long_spec = of_long((1, heads, TILE, TILE), half)
    shape = jax.ShapeDtypeStruct
    first, qkv, probs_short, probs_long, mixed = pl.pallas_call(
        functools.partial(forward_attention, half, width, n),
        grid=(grid,),
        in_specs=[on_scalars(), short_spec, long_spec, kept((8, width)), kept((8, width))] + first_specs,
        out_specs=[
            by_step(tile),
            by_step((TILE, 3 * width)),
            probs_short_spec,
            probs_long_spec,
            by_step(tile),
        ],
        out_shape=[
            shape((total, width), bfloat),
            shape((total, 3 * width), bfloat),
            shape((n_short, heads, 128, 128), bfloat),
            shape((n_long, heads, TILE, TILE), bfloat),
            shape((total, width), bfloat),
        ],
        scratch_shapes=[pltpu.VMEM((width, 3 * width), bfloat), pltpu.VMEM((1, 3 * width), single)],
        compiler_params=params(),
        cost_estimate=cost(2 * total * width * 3 * width * 2, total * width * 40),
        name="forward_attention",
    )(place, short, long, embed, smalls, *first_pieces)

    owners = width // rows
    if count == SHARDS:
        down_line, up_other, up_core, mixed = tie(down_line, up_other, up_core, mixed)
        up_pieces = [up_line, up_other, up_core, across(up_other, 1)]
        down_line = jnp.stack(down_line)
        down_line, up_pieces = tie(down_line, up_pieces)
        down_core, down_other = across(down_line, 1), across(down_line, 2)
    middle, second, active, slope, up_whole = pl.pallas_call(
        functools.partial(forward_up, half, width, hidden, len(up_pieces)),
        grid=(grid,),
        in_specs=[
            on_scalars(),
            short_spec,
            long_spec,
            kept((8, width)),
            kept((8, width)),
            kept((1, hidden)),
            by_step(tile),
        ]
        + [resident(p.shape) for p in up_pieces],
        out_specs=[
            by_step(tile),
            by_step(tile),
            by_step((TILE, hidden)),
            by_step((TILE, hidden)),
            kept((width, width + hidden)),
        ],
        out_shape=[
            shape((total, width), single),
            shape((total, width), bfloat),
            shape((total, hidden), bfloat),
            shape((total, hidden), bfloat),
            shape((width, width + hidden), bfloat),
        ],
        compiler_params=params(),
        cost_estimate=cost(2 * total * width * (width + hidden) * 2, total * width * 20),
        name="forward_up",
    )(place, short, long, embed, smalls, bias, mixed, *up_pieces)

    slots = SHARDS // 2
    whole_rows = width // SHARDS
    down_terms = pl.pallas_call(
        down_weight_back,
        grid=(hidden // width,),
        in_specs=[
            pl.BlockSpec((total, width), lambda i: (0, i)),
            kept(up_short.shape),
            kept(up_long.shape),
        ],
        out_specs=by_step((width, width)),
        out_shape=shape((hidden, width), bfloat),
        compiler_params=params(),
        cost_estimate=cost(2 * total * width * hidden, total * width * 12),
        name="down_weight_back",
    )(active, up_short, up_long)
    down_share = lax.psum_scatter(down_terms, "fsdp", scatter_dimension=0, tiled=True)
    if count == SHARDS:
        down_terms, slope, down_other = tie(down_terms, slope, down_other)
        down_pieces = [down_line, down_other, down_core, across(down_other, 1)]

    hidden_grad, branch, middle_grad, mixed_grad, down_whole, vectors, bias_grad = pl.pallas_call(
        functools.partial(feed_back, half, width, hidden, len(down_pieces)),
        grid=(grid,),
        in_specs=[
            on_scalars(),
            short_spec,
            long_spec,
            by_step((TILE, hidden)),
            by_step(tile),
            kept((8, width)),
            resident(up_whole.shape),
        ]
        + [resident(p.shape) for p in down_pieces],
        out_specs=[
            by_step((TILE, hidden)),
            by_step(tile),
            by_step(tile),
            by_step(tile),
            kept((hidden, width)),
            kept((8, width)),
            kept((1, hidden)),
        ],
        out_shape=[
            shape((total, hidden), bfloat),
            shape((total, width), bfloat),
            shape((total, width), single),
            shape((total, width), bfloat),
            shape((hidden, width), bfloat),
            shape((8, width), single),
            shape((1, hidden), single),
        ],
        scratch_shapes=[pltpu.VMEM(tile, bfloat)],
        compiler_params=params(),
        cost_estimate=cost(2 * total * width * (width + 2 * hidden), total * width * 30),
        name="feed_back",
    )(place, up_short, up_long, slope, middle, smalls, up_whole, *down_pieces)

    tiles = hidden // width
    column = lambda last: pl.BlockSpec((total, width), lambda i: (0, jnp.minimum(i, last)))
    out_block = pl.BlockSpec((slots, whole_rows, width), lambda i: (0, 0, i))
    up_keep, up_send = pl.pallas_call(
        functools.partial(weight_back, (1, tiles)),
        grid=(tiles + 1,),
        in_specs=[
            on_scalars(),
            kept((total, width)),
            kept((total, width)),
            kept((total, width)),
            pl.BlockSpec((total, width), lambda i: (0, jnp.maximum(i - 1, 0))),
        ],
        out_specs=[out_block] * 2,
        out_shape=[shape((slots, whole_rows, width + hidden), bfloat)] * 2,
        compiler_params=params(),
        cost_estimate=cost(2 * total * width * (width + hidden), total * width * 20),
        name="up_weight_back",
    )(place, mixed, second, branch, hidden_grad)
    up_sum = Scatter(count, up_keep, up_send)
    (qkv,) = up_sum.over_y(qkv)

    projected_grad = pl.pallas_call(
        functools.partial(backward_attention, half, width),
        grid=(grid,),
        in_specs=[by_step((TILE, 3 * width)), by_step(tile), probs_short_spec, probs_long_spec],
        out_specs=by_step((TILE, 3 * width)),
        out_shape=shape((total, 3 * width), bfloat),
        compiler_params=params(),
        cost_estimate=cost(2 * total * width * 3 * width * 2, total * width * 20),
        name="backward_attention",
    )(qkv, mixed_grad, probs_short, probs_long)

    qkv_keep, qkv_send = pl.pallas_call(
        functools.partial(weight_back, (3,)),
        grid=(3,),
        in_specs=[on_scalars(), kept((total, width)), column(2)],
        out_specs=[out_block] * 2,
        out_shape=[shape((slots, whole_rows, 3 * width), bfloat)] * 2,
        compiler_params=params(),
        cost_estimate=cost(2 * total * width * 3 * width, total * width * 16),
        name="qkv_weight_back",
    )(place, first, projected_grad)
    qkv_sum = Scatter(count, qkv_keep, qkv_send)
    middle_grad, qkv_sum.keep, down_share = up_sum.over_z(middle_grad, qkv_sum.keep, down_share)
    (middle_grad,) = qkv_sum.over_y(middle_grad)

    grad_short, grad_long, last_vectors, sums = pl.pallas_call(
        functools.partial(start_back, half, width, n),
        grid=(grid,),
        in_specs=[
            on_scalars(),
            short_spec,
            long_spec,
            kept((8, width)),
            kept((8, width)),
            by_step(tile),
            by_step((TILE, 3 * width)),
        ]
        + first_specs,
        out_specs=[short_spec, long_spec, kept((8, width)), kept((8, width))],
        out_shape=[
            shape(short.shape, bfloat),
            shape(long.shape, bfloat),
            shape((8, width), single),
            shape((8, width), single),
        ],
        scratch_shapes=[pltpu.VMEM((width, 3 * width), bfloat)],
        compiler_params=params(),
        cost_estimate=cost(2 * total * width * 3 * width, total * width * 30),
        name="start_back",
    )(place, short, long, embed, smalls, middle_grad, projected_grad, *first_pieces)
    middle, sums = tie(middle, sums)
    output_short, output_long = pl.pallas_call(
        functools.partial(forward_down, half),
        grid=(grid,),
        in_specs=[by_step(tile), by_step((TILE, hidden)), kept((8, width)), resident(down_whole.shape)],
        out_specs=[short_spec, long_spec],
        out_shape=[shape(short.shape, bfloat), shape(long.shape, bfloat)],
        compiler_params=params(),
        cost_estimate=cost(2 * total * width * hidden, total * width * 30),
        name="forward_down",
    )(middle, active, smalls, down_whole)

    owners = width // rows
    both = jnp.concatenate([vectors[:4], last_vectors[:4], sums[:marks]], axis=0)
    lines = both.shape[0]
    packed = both.reshape(lines, owners, rows).transpose(1, 0, 2).reshape(owners, lines * rows)
    own_steps = jnp.broadcast_to(steps.astype(single), (owners, marks))
    packed = jnp.concatenate([packed, bias_grad.reshape(owners, -1), own_steps], axis=1)
    packed = jnp.concatenate([packed, packed], axis=0)
    came = lax.all_to_all(packed, ("rep", "fsdp"), 0, 0, tiled=True)
    output_short, came, up_sum.keep = qkv_sum.over_z(output_short, came, up_sum.keep)
    vector_sums = jnp.sum(came[:, : 8 * rows], axis=0).reshape(8, rows)
    ends = lines * rows + hidden // owners
    up_bias_grad = jnp.sum(came[:, lines * rows : ends], axis=0)
    sequence_sums = came[:, 8 * rows : lines * rows].reshape(-1, rows)
    all_steps = came[:, ends:].astype(jnp.int32).reshape(-1)
    selector = (all_steps[:, None] == jnp.arange(timesteps, dtype=jnp.int32)[None, :]).astype(single)
    table_grad = lax.dot_general(
        selector,
        sequence_sums,
        TN,
        precision=lax.Precision.HIGHEST,
        preferred_element_type=single,
    )
    up_sum.over_x()
    qkv_sum.over_x()
    up_grads, qkv_weight_grad = up_sum.result(), qkv_sum.result()
    down_weight_grad = added(down_share, to_replica(down_share))
    return (
        output_short.reshape(input_short.shape),
        output_long.reshape(input_long.shape),
        grad_short.reshape(input_short.shape),
        grad_long.reshape(input_long.shape),
        table_grad,
        vector_sums[4],
        vector_sums[5],
        qkv_weight_grad,
        vector_sums[6],
        vector_sums[7],
        up_grads[:, :width],
        vector_sums[2],
        vector_sums[0],
        vector_sums[1],
        up_grads[:, width:],
        up_bias_grad,
        down_weight_grad,
        vector_sums[3],
    )


def solution(mesh):
    rows = P(("rep", "fsdp"), None, None)
    steps = P(("rep", "fsdp"))
    vector, matrix, table = P("fsdp"), P("fsdp", None), P(None, "fsdp")
    weights = (
        table,
        vector,
        vector,
        matrix,
        vector,
        vector,
        matrix,
        vector,
        vector,
        vector,
        matrix,
        vector,
        matrix,
        vector,
    )
    return jax.shard_map(
        functools.partial(shards, mesh.shape["fsdp"]),
        mesh=mesh,
        in_specs=(rows, rows, steps, steps, rows, rows) + weights,
        out_specs=(rows,) * 4 + weights,
        check_vma=False,
    )
```

```python
import functools

import jax
import jax.numpy as jnp
from jax import lax
from jax.experimental import pallas as pl
from jax.experimental.pallas import tpu as pltpu
from jax.sharding import PartitionSpec as P

bfloat = jnp.bfloat16
single = jnp.float32

HEAD_DIM = 64
PAIR = 2 * HEAD_DIM
TILE = 256
BAND = 256
SHORT = 128
LONG = 256
SHARDS = 16
LOG2E = 1.4426950408889634
GELU_A = 0.7978845608028654
GELU_B = GELU_A * 0.044715

NN = (((1,), (0,)), ((), ()))
NT = (((1,), (1,)), ((), ()))
TN = (((0,), (0,)), ((), ()))


def dot(left, right, dims):
    return lax.dot_general(left, right, dims, preferred_element_type=single)


def params(vmem=56 << 20):
    return pltpu.CompilerParams(vmem_limit_bytes=vmem)


def cost(flops, moved):
    return pl.CostEstimate(flops=1024, bytes_accessed=1024, transcendentals=0)


def resident(shape):
    zeros = (0,) * len(shape)
    return pl.BlockSpec(shape, lambda *_: zeros, pipeline_mode=pl.Buffered(1))


def kept(shape):
    zeros = (0,) * len(shape)
    return pl.BlockSpec(shape, lambda *_: zeros)


def of_short(shape, half):
    tail = (0,) * (len(shape) - 1)
    return pl.BlockSpec(shape, lambda i: (jnp.minimum(i, half - 1),) + tail)


def of_long(shape, half):
    tail = (0,) * (len(shape) - 1)
    return pl.BlockSpec(shape, lambda i: (jnp.maximum(i - half, 0),) + tail)


def by_step(shape):
    tail = (0,) * (len(shape) - 1)
    return pl.BlockSpec(shape, lambda i: (i,) + tail)


def on_scalars():
    return pl.BlockSpec(memory_space=pltpu.SMEM)


def assemble(place, pieces, out_ref):
    columns = out_ref.shape[1]
    for i, piece in enumerate(pieces):
        rows = piece.shape[0]
        at = pl.multiple_of((place ^ i) * rows, rows)
        out_ref[pl.ds(at, rows), :] = piece[:, :columns]


def assemble_lines(place, pieces, out_ref):
    for piece, low in zip(pieces, (0, 2, 1, 3)):
        rows = piece.shape[1]
        for z in range(piece.shape[0]):
            at = pl.multiple_of((place ^ (z << 2 | low)) * rows, rows)
            out_ref[pl.ds(at, rows), :] = piece[z]


def standardize(rows):
    centre = rows - jnp.mean(rows, axis=-1, keepdims=True)
    factor = lax.rsqrt(jnp.mean(centre * centre, axis=-1, keepdims=True) + 1e-05)
    return centre * factor, factor


def norm_back(upper, scaled, factor, gain):
    inner = upper * gain
    return factor * (
        inner
        - jnp.mean(inner, axis=-1, keepdims=True)
        - scaled * jnp.mean(inner * scaled, axis=-1, keepdims=True)
    )


def start_rows(step, half, size, short_ref, long_ref, embed_ref, emit):
    def group(rows_ref, length, number, is_short):
        rows = rows_ref[...].astype(single)
        parts = []
        for s in range(size // length):
            embed = embed_ref[pl.ds(number + s, 1), :]
            parts.append(rows[s * length : (s + 1) * length] + embed)
        emit(parts[0] if len(parts) == 1 else jnp.concatenate(parts, axis=0), is_short)

    @pl.when(step < half)
    def _():
        group(short_ref, SHORT, step * (size // SHORT), True)

    @pl.when(step >= half)
    def _():
        group(long_ref, LONG, half * (size // SHORT) + (step - half) * (size // LONG), False)


def attend(query, keys, values, probs_ref, at):
    first_half = lax.broadcasted_iota(jnp.int32, (1, PAIR), 1) < HEAD_DIM
    turned = values.T
    parts = []
    for j in range(2):
        own = first_half if j == 0 else jnp.logical_not(first_half)
        masked = jnp.where(own, keys, jnp.zeros_like(keys))
        scores = dot(masked, query, NT)
        summit = jnp.max(scores, axis=0, keepdims=True)
        expo = jnp.exp2((scores - summit) * (LOG2E * HEAD_DIM ** (-0.5)))
        total = jnp.sum(expo, axis=0, keepdims=True)
        probs = (expo * (1.0 / total)).astype(bfloat)
        probs_ref[at[0], at[1] + j] = probs
        parts.append(dot(turned[j * HEAD_DIM : (j + 1) * HEAD_DIM], probs, NN))
    return jnp.concatenate(parts, axis=0).T


def forward_attention(
    half, width, n_pieces, place_ref, short_ref, long_ref, embed_ref, small_ref, *refs
):
    pieces = refs[:n_pieces]
    first_ref, qkv_ref, probs_short, probs_long, mixed_ref, weight, joined = refs[n_pieces:]
    step = pl.program_id(0)
    heads = width // HEAD_DIM

    @pl.when(step == 0)
    def _():
        place = place_ref[0]
        assemble(place, pieces, weight)
        joined[...] = jnp.zeros_like(joined)
        joined[:, 0:width] = small_ref[2:3]
        joined[:, 2 * width :] = small_ref[3:4]

    def emit(start, is_short):
        scaled, _ = standardize(start)
        first = (scaled * small_ref[0:1, :] + small_ref[1:2, :]).astype(bfloat)
        first_ref[...] = first
        for part in range(3):
            cols = slice(part * width, (part + 1) * width)
            qkv_ref[:, cols] = (dot(first, weight[:, cols], NN) + joined[:, cols]).astype(bfloat)
        length = 128 if is_short else TILE
        probs_ref = probs_short if is_short else probs_long
        for s in range(TILE // length):
            rows = slice(s * length, (s + 1) * length)
            for pair in range(heads // 2):
                cols = slice(pair * PAIR, (pair + 1) * PAIR)
                query = qkv_ref[rows, cols]
                keys = qkv_ref[rows, width + pair * PAIR : width + (pair + 1) * PAIR]
                values = qkv_ref[rows, 2 * width + pair * PAIR : 2 * width + (pair + 1) * PAIR]
                mixed_ref[rows, cols] = attend(query, keys, values, probs_ref, (s, 2 * pair)).astype(
                    bfloat
                )

    start_rows(step, half, short_ref.shape[0], short_ref, long_ref, embed_ref, emit)


def forward_up(
    half, width, hidden, n_up, place_ref, short_ref, long_ref, embed_ref, small_ref, bias_ref, mixed_ref, *refs
):
    ups = refs[:n_up]
    middle_ref, second_ref, active_ref, slope_ref, weight = refs[n_up:]
    step = pl.program_id(0)

    @pl.when(step == 0)
    def _():
        assemble_lines(place_ref[0], ups, weight)

    def emit(start, _):
        middle_ref[...] = start

    start_rows(step, half, short_ref.shape[0], short_ref, long_ref, embed_ref, emit)
    middle = middle_ref[...] + dot(mixed_ref[...], weight[:, :width], NN) + small_ref[4:5, :]
    middle_ref[...] = middle
    scaled, _ = standardize(middle)
    second = (scaled * small_ref[5:6, :] + small_ref[6:7, :]).astype(bfloat)
    second_ref[...] = second
    for at in range(0, hidden, width):
        cols = slice(at, at + width)
        u = dot(second, weight[:, width + at : 2 * width + at], NN) + bias_ref[:, cols]
        square = u * u
        half_up = 0.5 + 0.5 * jnp.tanh(u * (GELU_A + GELU_B * square))
        active = u * half_up
        active_ref[:, cols] = active.astype(bfloat)
        slope = half_up + active * (1.0 - half_up) * (2.0 * GELU_A + 6.0 * GELU_B * square)
        slope_ref[:, cols] = slope.astype(bfloat)


def store_shard(place, shard, value, keep_ref, send_ref):
    rel = place ^ shard
    slot = ((rel >> 1) & 1) * 4 + (rel >> 2)

    @pl.when((rel & 1) == 0)
    def _():
        keep_ref[slot] = value

    @pl.when((rel & 1) == 1)
    def _():
        send_ref[slot] = value


def down_weight_back(active_ref, short_ref, long_ref, out_ref, grad):
    @pl.when(pl.program_id(0) == 0)
    def _():
        split = short_ref.shape[0]
        grad[:split, :] = short_ref[...]
        grad[split:, :] = long_ref[...]

    out_ref[...] = dot(active_ref[...], grad[...], TN).astype(bfloat)


def weight_back(parts, place_ref, *refs):
    lefts, rights = refs[: len(parts)], refs[len(parts) : 2 * len(parts)]
    keep_ref, send_ref, turned = refs[2 * len(parts) :]
    step = pl.program_id(0)
    place = place_ref[0]
    rows = keep_ref.shape[1]
    begin = 0
    for left_ref, right_ref, tiles in zip(lefts, rights, parts):

        @pl.when(step == begin)
        def _(left_ref=left_ref):
            turned[...] = left_ref[...].T

        def work(right_ref=right_ref):
            total = dot(turned[...], right_ref[...], NN).astype(bfloat)
            for k in range(SHARDS):
                store_shard(place, k, total[k * rows : (k + 1) * rows], keep_ref, send_ref)

        if len(parts) == 1:
            work()
        else:
            pl.when(jnp.logical_and(step >= begin, step < begin + tiles))(work)
        begin += tiles


def feed_back(
    half, width, hidden, n, place_ref, short_ref, long_ref, slope_ref, middle_ref, small_ref, *refs
):
    ups, downs = refs[:n], refs[n : 2 * n]
    (hidden_grad_ref, branch_ref, middle_grad_ref, mixed_grad_ref, vector_ref, bias_ref, weight, down, grad) = refs[
        2 * n :
    ]
    step = pl.program_id(0)

    @pl.when(step == 0)
    def _():
        assemble_lines(place_ref[0], ups, weight)
        assemble_lines(place_ref[0], downs, down)
        vector_ref[...] = jnp.zeros_like(vector_ref)
        bias_ref[...] = jnp.zeros_like(bias_ref)

    @pl.when(step < half)
    def _():
        grad[...] = short_ref[...]

    @pl.when(step >= half)
    def _():
        grad[...] = long_ref[...]

    upper = jnp.zeros((grad.shape[0], width), single)
    for at in range(0, hidden, width):
        cols = slice(at, at + width)
        passed = dot(grad[...], down[cols, :], NT) * slope_ref[:, cols].astype(single)
        low = passed.astype(bfloat)
        hidden_grad_ref[:, cols] = low
        bias_ref[:, cols] += jnp.sum(low.astype(single), axis=0, keepdims=True)
        upper += dot(low, weight[:, width + at : 2 * width + at], NT)
    scaled, factor = standardize(middle_ref[...])
    rows = grad[...].astype(single)
    middle_grad = rows + norm_back(upper, scaled, factor, small_ref[5:6, :])
    middle_grad_ref[...] = middle_grad
    branch = middle_grad.astype(bfloat)
    branch_ref[...] = branch
    mixed_grad_ref[...] = dot(branch, weight[:, :width], NT).astype(bfloat)
    vector_ref[0:1, :] += jnp.sum(upper * scaled, axis=0, keepdims=True)
    vector_ref[1:2, :] += jnp.sum(upper, axis=0, keepdims=True)
    vector_ref[2:3, :] += jnp.sum(branch.astype(single), axis=0, keepdims=True)
    vector_ref[3:4, :] += jnp.sum(rows, axis=0, keepdims=True)


def attend_back(query, keys, values, upper, probs_ref, at):
    first_half = lax.broadcasted_iota(jnp.int32, (1, PAIR), 1) < HEAD_DIM
    turned = keys.T
    value_parts, key_parts, query_parts = [], [], []
    for j in range(2):
        own = first_half if j == 0 else jnp.logical_not(first_half)
        masked = jnp.where(own, values, jnp.zeros_like(values))
        probs = probs_ref[at[0], at[1] + j]
        wide = probs.astype(single)
        probs_grad = dot(masked, upper, NT)
        inner = jnp.sum(wide * probs_grad, axis=0, keepdims=True)
        scores_grad = (wide * (probs_grad - inner)).astype(bfloat)
        value_parts.append(dot(probs, upper, NN))
        key_parts.append(dot(scores_grad, query, NN))
        query_parts.append(dot(turned[j * HEAD_DIM : (j + 1) * HEAD_DIM], scores_grad, NN))
    scale = HEAD_DIM ** (-0.5)
    query_grad = jnp.concatenate(query_parts, axis=0).T * scale
    keys_grad = jnp.where(first_half, key_parts[0], key_parts[1]) * scale
    values_grad = jnp.where(first_half, value_parts[0], value_parts[1])
    return query_grad.astype(bfloat), keys_grad.astype(bfloat), values_grad.astype(bfloat)


def backward_attention(half, width, qkv_ref, mixed_grad_ref, probs_short, probs_long, grad_ref):
    step = pl.program_id(0)
    heads = width // HEAD_DIM

    def group(length, probs_ref):
        for s in range(TILE // length):
            rows = slice(s * length, (s + 1) * length)
            for pair in range(heads // 2):
                spots = [slice(part * width + pair * PAIR, part * width + (pair + 1) * PAIR) for part in range(3)]
                query, keys, values = (qkv_ref[rows, spot] for spot in spots)
                upper = mixed_grad_ref[rows, spots[0]]
                for spot, value in zip(spots, attend_back(query, keys, values, upper, probs_ref, (s, 2 * pair))):
                    grad_ref[rows, spot] = value

    pl.when(step < half)(lambda: group(128, probs_short))
    pl.when(step >= half)(lambda: group(TILE, probs_long))


def start_back(
    half, width, n_first, place_ref, short_ref, long_ref, embed_ref, small_ref, middle_grad_ref, grad_ref, *refs
):
    firsts = refs[:n_first]
    in_short, in_long, vector_ref, sums_ref, weight = refs[n_first:]
    step = pl.program_id(0)
    size = short_ref.shape[0]

    @pl.when(step == 0)
    def _():
        assemble(place_ref[0], firsts, weight)
        vector_ref[...] = jnp.zeros_like(vector_ref)
        sums_ref[...] = jnp.zeros_like(sums_ref)

    def emit(start, is_short):
        upper = dot(grad_ref[...], weight[...], NT)
        scaled, factor = standardize(start)
        start_grad = middle_grad_ref[...] + norm_back(upper, scaled, factor, small_ref[0:1, :])
        vector_ref[0:1, :] += jnp.sum(upper * scaled, axis=0, keepdims=True)
        vector_ref[1:2, :] += jnp.sum(upper, axis=0, keepdims=True)
        vector_ref[2:3, :] += jnp.sum(grad_ref[:, :width].astype(single), axis=0, keepdims=True)
        vector_ref[3:4, :] += jnp.sum(grad_ref[:, 2 * width :].astype(single), axis=0, keepdims=True)
        out, length = (in_short, SHORT) if is_short else (in_long, LONG)
        out[...] = start_grad.astype(bfloat)
        number = step * (size // SHORT) if is_short else half * (size // SHORT) + (step - half) * (size // LONG)
        for s in range(size // length):
            sums_ref[pl.ds(number + s, 1), :] = jnp.sum(
                start_grad[s * length : (s + 1) * length], axis=0, keepdims=True
            )

    start_rows(step, half, short_ref.shape[0], short_ref, long_ref, embed_ref, emit)


def forward_down(half, n, place_ref, middle_ref, active_ref, small_ref, *refs):
    downs, (out_short, out_long, down) = refs[:n], refs[n:]
    step = pl.program_id(0)

    @pl.when(step == 0)
    def _():
        assemble_lines(place_ref[0], downs, down)

    result = middle_ref[...] + dot(active_ref[...], down[...], NN) + small_ref[7:8, :]

    @pl.when(step < half)
    def _():
        out_short[...] = result.astype(bfloat)

    @pl.when(step >= half)
    def _():
        out_long[...] = result.astype(bfloat)


def flip(bit):
    return [(i, i ^ bit) for i in range(SHARDS)]


def across(array, bit):
    return lax.ppermute(array, "fsdp", flip(bit))


def to_replica(array):
    return lax.ppermute(array, "rep", [(0, 1), (1, 0)])


def tie(*values):
    return lax.optimization_barrier(values)


def spread(line, other):
    others = [other] + [across(piece, 2) for piece in line[1:]]
    pieces = []
    for held in zip(line, others):
        for piece in held:
            pieces += [piece, across(piece, 1)]
    return pieces


def along(shard):
    return [shard] + [across(shard, z << 2) for z in (1, 2, 3)]


def added(*terms):
    total = terms[0].astype(single)
    for term in terms[1:]:
        total = total + term.astype(single)
    return total


class Scatter:
    def __init__(self, count, keep, send):
        self.count = count
        self.keep = keep
        if count == SHARDS:
            self.came = across(send, 1)
        else:
            both = jnp.stack([keep, send]).reshape((2, 2, 4) + keep.shape[1:])
            whole = both.transpose(2, 1, 0, 3, 4).reshape(-1, keep.shape[2])
            self.share = lax.psum_scatter(whole, "fsdp", scatter_dimension=0, tiled=True)

    def over_y(self, *after):
        if self.count != SHARDS:
            return after
        self.keep, self.came, after = tie(self.keep, self.came, after)
        theirs = added(self.keep[4:], self.came[4:]).astype(bfloat)
        self.keep = added(self.keep[:4], self.came[:4]).astype(bfloat)
        theirs, after = tie(theirs, after)
        self.came = across(theirs, 2)
        return after

    def over_z(self, *after):
        if self.count != SHARDS:
            return after
        self.keep, self.came, after = tie(self.keep, self.came, after)
        slots = [added(self.keep[z], self.came[z]) for z in range(4)]
        self.keep = slots[0].astype(bfloat)
        lows, after = tie([slot.astype(bfloat) for slot in slots[1:]], after)
        self.came = [across(low, (z + 1) << 2) for z, low in enumerate(lows)]
        return after

    def over_x(self, *after):
        if self.count == SHARDS:
            terms, after = tie([self.keep] + self.came, after)
            self.share = added(*terms).astype(bfloat)
        else:
            self.share = self.share.astype(bfloat)
        self.share, after = tie(self.share, after)
        self.other = to_replica(self.share)
        return after

    def result(self):
        return added(self.share, self.other)


def shards(
    count,
    input_short,
    input_long,
    steps_short,
    steps_long,
    upstream_short,
    upstream_long,
    step_table,
    attn_gain,
    attn_shift,
    qkv_weight,
    query_bias,
    value_bias,
    out_weight,
    out_bias,
    ffn_gain,
    ffn_shift,
    up_weight,
    up_bias,
    down_weight,
    down_bias,
):
    width, rows = out_weight.shape[1], out_weight.shape[0]
    hidden = up_weight.shape[1]
    n_short, n_long = steps_short.shape[0], steps_long.shape[0]
    short = input_short.reshape(-1, width)
    long = input_long.reshape(-1, width)
    up_short = upstream_short.reshape(-1, width)
    up_long = upstream_long.reshape(-1, width)
    total = short.shape[0] + long.shape[0]
    grid = total // TILE
    half = short.shape[0] // TILE
    heads = width // HEAD_DIM
    timesteps = step_table.shape[0]

    first_shard = qkv_weight.astype(bfloat)
    up_shard = jnp.concatenate([out_weight, up_weight], axis=1).astype(bfloat)
    down_shard = down_weight.astype(bfloat)

    place = (lax.axis_index("fsdp") if count == SHARDS else jnp.int32(0)).reshape(1).astype(jnp.int32)
    owners = width // rows
    steps = jnp.concatenate([steps_short, steps_long])
    marks = steps.shape[0]
    vectors = [attn_gain, attn_shift, query_bias, value_bias, out_bias, ffn_gain, ffn_shift, down_bias]
    own = jnp.concatenate(vectors + [up_bias]).astype(bfloat)
    told = lax.all_to_all(jnp.broadcast_to(steps, (owners, marks)), "fsdp", 0, 0, tiled=True)
    if count == SHARDS:
        shard_z = along(first_shard)
        shard_y = across(first_shard, 2)
        told, shard_z, shard_y = tie(told, shard_z, shard_y)
    chosen = (told.reshape(-1, 1) == jnp.arange(timesteps, dtype=jnp.int32)).astype(bfloat)
    chosen = jnp.dot(chosen, step_table.astype(bfloat), preferred_element_type=single).astype(bfloat)
    chosen = chosen.reshape(owners, marks * rows)
    chosen = jnp.concatenate([chosen, jnp.broadcast_to(own, (owners, own.shape[0]))], axis=1)
    told = lax.all_to_all(chosen, "fsdp", 0, 0, tiled=True)
    most = (marks + 8) * rows
    told = told.astype(single)
    rest = told[:, :most].reshape(owners, marks + 8, rows).transpose(1, 0, 2).reshape(marks + 8, width)
    embed = jnp.pad(rest[:marks], ((0, 8 - marks), (0, 0)))
    smalls = rest[marks:]
    bias = told[:, most:].reshape(1, hidden)
    if count == SHARDS:
        up_shard, shard_y = tie(up_shard, shard_y)
        first_pieces = spread(shard_z, shard_y)
        up_line, others, embed, smalls, bias = tie(
            along(up_shard), [first_pieces[i] for i in (6, 10, 14)], embed, smalls, bias
        )
        first_pieces[6], first_pieces[10], first_pieces[14] = others
        up_line = jnp.stack(up_line)
        up_line, down_shard, first_pieces[-1] = tie(up_line, down_shard, first_pieces[-1])
        up_core, up_other = across(up_line, 1), across(up_line, 2)
        down_line = along(down_shard)
    else:
        first_pieces = [lax.all_gather(first_shard, "fsdp", axis=0, tiled=True)]
        up_pieces = [lax.all_gather(up_shard, "fsdp", axis=0, tiled=True)[None]]
        down_pieces = [lax.all_gather(down_shard, "fsdp", axis=0, tiled=True)[None]]
    n = len(first_pieces)
    first_specs = [resident(p.shape) for p in first_pieces]

    tile = (TILE, width)
    short_spec, long_spec = of_short(tile, half), of_long(tile, half)
    band, half_band = (BAND, width), short.shape[0] // BAND
    short_band, long_band = of_short(band, half_band), of_long(band, half_band)
    probs_short_spec = of_short((TILE // 128, heads, 128, 128), half)
    probs_long_spec = of_long((1, heads, TILE, TILE), half)
    shape = jax.ShapeDtypeStruct
    first, qkv, probs_short, probs_long, mixed = pl.pallas_call(
        functools.partial(forward_attention, half, width, n),
        grid=(grid,),
        in_specs=[on_scalars(), short_spec, long_spec, kept((8, width)), kept((8, width))] + first_specs,
        out_specs=[
            by_step(tile),
            by_step((TILE, 3 * width)),
            probs_short_spec,
            probs_long_spec,
            by_step(tile),
        ],
        out_shape=[
            shape((total, width), bfloat),
            shape((total, 3 * width), bfloat),
            shape((n_short, heads, 128, 128), bfloat),
            shape((n_long, heads, TILE, TILE), bfloat),
            shape((total, width), bfloat),
        ],
        scratch_shapes=[pltpu.VMEM((width, 3 * width), bfloat), pltpu.VMEM((1, 3 * width), single)],
        compiler_params=params(),
        cost_estimate=cost(2 * total * width * 3 * width * 2, total * width * 40),
        name="forward_attention",
    )(place, short, long, embed, smalls, *first_pieces)

    owners = width // rows
    if count == SHARDS:
        down_line, up_other, up_core, mixed = tie(down_line, up_other, up_core, mixed)
        up_pieces = [up_line, up_other, up_core, across(up_other, 1)]
        down_line = jnp.stack(down_line)
        down_line, up_pieces = tie(down_line, up_pieces)
        down_core, down_other = across(down_line, 1), across(down_line, 2)
    middle, second, active, slope = pl.pallas_call(
        functools.partial(forward_up, half_band, width, hidden, len(up_pieces)),
        grid=(total // BAND,),
        in_specs=[
            on_scalars(),
            short_band,
            long_band,
            kept((8, width)),
            kept((8, width)),
            kept((1, hidden)),
            by_step(band),
        ]
        + [resident(p.shape) for p in up_pieces],
        out_specs=[
            by_step(band),
            by_step(band),
            by_step((BAND, hidden)),
            by_step((BAND, hidden)),
        ],
        out_shape=[
            shape((total, width), single),
            shape((total, width), bfloat),
            shape((total, hidden), bfloat),
            shape((total, hidden), bfloat),
        ],
        scratch_shapes=[pltpu.VMEM((width, width + hidden), bfloat)],
        compiler_params=params(),
        cost_estimate=cost(2 * total * width * (width + hidden) * 2, total * width * 20),
        name="forward_up",
    )(place, short, long, embed, smalls, bias, mixed, *up_pieces)

    slots = SHARDS // 2
    whole_rows = width // SHARDS
    down_terms = pl.pallas_call(
        down_weight_back,
        grid=(hidden // width,),
        in_specs=[
            pl.BlockSpec((total, width), lambda i: (0, i)),
            kept(up_short.shape),
            kept(up_long.shape),
        ],
        out_specs=by_step((width, width)),
        out_shape=shape((hidden, width), bfloat),
        scratch_shapes=[pltpu.VMEM((total, width), bfloat)],
        compiler_params=params(),
        cost_estimate=cost(2 * total * width * hidden, total * width * 12),
        name="down_weight_back",
    )(active, up_short, up_long)
    down_share = lax.psum_scatter(down_terms, "fsdp", scatter_dimension=0, tiled=True)
    if count == SHARDS:
        down_terms, slope, down_other = tie(down_terms, slope, down_other)
        down_pieces = [down_line, down_other, down_core, across(down_other, 1)]

    hidden_grad, branch, middle_grad, mixed_grad, vectors, bias_grad = pl.pallas_call(
        functools.partial(feed_back, half_band, width, hidden, len(down_pieces)),
        grid=(total // BAND,),
        in_specs=[
            on_scalars(),
            short_band,
            long_band,
            by_step((BAND, hidden)),
            by_step(band),
            kept((8, width)),
        ]
        + [resident(p.shape) for p in [*up_pieces, *down_pieces]],
        out_specs=[
            by_step((BAND, hidden)),
            by_step(band),
            by_step(band),
            by_step(band),
            kept((8, width)),
            kept((1, hidden)),
        ],
        out_shape=[
            shape((total, hidden), bfloat),
            shape((total, width), bfloat),
            shape((total, width), single),
            shape((total, width), bfloat),
            shape((8, width), single),
            shape((1, hidden), single),
        ],
        scratch_shapes=[
            pltpu.VMEM((width, width + hidden), bfloat),
            pltpu.VMEM((hidden, width), bfloat),
            pltpu.VMEM(band, bfloat),
        ],
        compiler_params=params(),
        cost_estimate=cost(2 * total * width * (width + 2 * hidden), total * width * 30),
        name="feed_back",
    )(place, up_short, up_long, slope, middle, smalls, *up_pieces, *down_pieces)

    tiles = hidden // width
    column = lambda last: pl.BlockSpec((total, width), lambda i: (0, jnp.minimum(i, last)))
    out_block = pl.BlockSpec((slots, whole_rows, width), lambda i: (0, 0, i))
    up_keep, up_send = pl.pallas_call(
        functools.partial(weight_back, (1, tiles)),
        grid=(tiles + 1,),
        in_specs=[
            on_scalars(),
            kept((total, width)),
            kept((total, width)),
            kept((total, width)),
            pl.BlockSpec((total, width), lambda i: (0, jnp.maximum(i - 1, 0))),
        ],
        out_specs=[out_block] * 2,
        out_shape=[shape((slots, whole_rows, width + hidden), bfloat)] * 2,
        scratch_shapes=[pltpu.VMEM((width, total), bfloat)],
        compiler_params=params(),
        cost_estimate=cost(2 * total * width * (width + hidden), total * width * 20),
        name="up_weight_back",
    )(place, mixed, second, branch, hidden_grad)
    up_sum = Scatter(count, up_keep, up_send)
    (qkv,) = up_sum.over_y(qkv)

    projected_grad = pl.pallas_call(
        functools.partial(backward_attention, half, width),
        grid=(grid,),
        in_specs=[by_step((TILE, 3 * width)), by_step(tile), probs_short_spec, probs_long_spec],
        out_specs=by_step((TILE, 3 * width)),
        out_shape=shape((total, 3 * width), bfloat),
        compiler_params=params(),
        cost_estimate=cost(2 * total * width * 3 * width * 2, total * width * 20),
        name="backward_attention",
    )(qkv, mixed_grad, probs_short, probs_long)

    qkv_keep, qkv_send = pl.pallas_call(
        functools.partial(weight_back, (3,)),
        grid=(3,),
        in_specs=[on_scalars(), kept((total, width)), column(2)],
        out_specs=[out_block] * 2,
        out_shape=[shape((slots, whole_rows, 3 * width), bfloat)] * 2,
        scratch_shapes=[pltpu.VMEM((width, total), bfloat)],
        compiler_params=params(),
        cost_estimate=cost(2 * total * width * 3 * width, total * width * 16),
        name="qkv_weight_back",
    )(place, first, projected_grad)
    qkv_sum = Scatter(count, qkv_keep, qkv_send)
    middle_grad, qkv_sum.keep, down_share = up_sum.over_z(middle_grad, qkv_sum.keep, down_share)
    (middle_grad,) = qkv_sum.over_y(middle_grad)

    grad_short, grad_long, last_vectors, sums = pl.pallas_call(
        functools.partial(start_back, half_band, width, n),
        grid=(total // BAND,),
        in_specs=[
            on_scalars(),
            short_band,
            long_band,
            kept((8, width)),
            kept((8, width)),
            by_step(band),
            by_step((BAND, 3 * width)),
        ]
        + first_specs,
        out_specs=[short_band, long_band, kept((8, width)), kept((8, width))],
        out_shape=[
            shape(short.shape, bfloat),
            shape(long.shape, bfloat),
            shape((8, width), single),
            shape((8, width), single),
        ],
        scratch_shapes=[pltpu.VMEM((width, 3 * width), bfloat)],
        compiler_params=params(),
        cost_estimate=cost(2 * total * width * 3 * width, total * width * 30),
        name="start_back",
    )(place, short, long, embed, smalls, middle_grad, projected_grad, *first_pieces)
    owners = width // rows
    both = jnp.concatenate([vectors[:4], last_vectors[:4], sums[:marks]], axis=0)
    lines = both.shape[0]
    packed = both.reshape(lines, owners, rows).transpose(1, 0, 2).reshape(owners, lines * rows)
    own_steps = jnp.broadcast_to(steps.astype(single), (owners, marks))
    packed = jnp.concatenate([packed, bias_grad.reshape(owners, -1), own_steps], axis=1)
    packed = jnp.concatenate([packed, packed], axis=0)
    came = lax.all_to_all(packed, ("rep", "fsdp"), 0, 0, tiled=True)
    if count == SHARDS:
        up_sum.came, qkv_sum.came, middle, came = tie(up_sum.came, qkv_sum.came, middle, came)
    middle, down_share = up_sum.over_x(middle, down_share)
    down_other = to_replica(down_share)
    (middle,) = qkv_sum.over_z(middle)
    output_short, output_long = pl.pallas_call(
        functools.partial(forward_down, half_band, len(down_pieces)),
        grid=(total // BAND,),
        in_specs=[on_scalars(), by_step(band), by_step((BAND, hidden)), kept((8, width))]
        + [resident(p.shape) for p in down_pieces],
        out_specs=[short_band, long_band],
        out_shape=[shape(short.shape, bfloat), shape(long.shape, bfloat)],
        scratch_shapes=[pltpu.VMEM((hidden, width), bfloat)],
        compiler_params=params(),
        cost_estimate=cost(2 * total * width * hidden, total * width * 30),
        name="forward_down",
    )(place, middle, active, smalls, *down_pieces)

    vector_sums = jnp.sum(came[:, : 8 * rows], axis=0).reshape(8, rows)
    ends = lines * rows + hidden // owners
    up_bias_grad = jnp.sum(came[:, lines * rows : ends], axis=0)
    sequence_sums = came[:, 8 * rows : lines * rows].reshape(-1, rows)
    all_steps = came[:, ends:].astype(jnp.int32).reshape(-1)
    selector = (all_steps[:, None] == jnp.arange(timesteps, dtype=jnp.int32)[None, :]).astype(single)
    table_grad = lax.dot_general(
        selector,
        sequence_sums,
        TN,
        precision=lax.Precision.HIGHEST,
        preferred_element_type=single,
    )
    down_other, up_sum.other = qkv_sum.over_x(down_other, up_sum.other)
    up_grads, qkv_weight_grad = up_sum.result(), qkv_sum.result()
    down_weight_grad = added(down_share, down_other)
    return (
        output_short.reshape(input_short.shape),
        output_long.reshape(input_long.shape),
        grad_short.reshape(input_short.shape),
        grad_long.reshape(input_long.shape),
        table_grad,
        vector_sums[4],
        vector_sums[5],
        qkv_weight_grad,
        vector_sums[6],
        vector_sums[7],
        up_grads[:, :width],
        vector_sums[2],
        vector_sums[0],
        vector_sums[1],
        up_grads[:, width:],
        up_bias_grad,
        down_weight_grad,
        vector_sums[3],
    )


def solution(mesh):
    rows = P(("rep", "fsdp"), None, None)
    steps = P(("rep", "fsdp"))
    vector, matrix, table = P("fsdp"), P("fsdp", None), P(None, "fsdp")
    weights = (
        table,
        vector,
        vector,
        matrix,
        vector,
        vector,
        matrix,
        vector,
        vector,
        vector,
        matrix,
        vector,
        matrix,
        vector,
    )
    return jax.shard_map(
        functools.partial(shards, mesh.shape["fsdp"]),
        mesh=mesh,
        in_specs=(rows, rows, steps, steps, rows, rows) + weights,
        out_specs=(rows,) * 4 + weights,
        check_vma=False,
    )
```

```python
import functools

import jax
import jax.numpy as jnp
from jax import lax
from jax.experimental import pallas as pl
from jax.experimental.pallas import tpu as pltpu
from jax.sharding import PartitionSpec as P

bfloat = jnp.bfloat16
single = jnp.float32

HEAD_DIM = 64
PAIR = 2 * HEAD_DIM
TILE = 256
BAND = 256
SHORT = 128
LONG = 256
SHARDS = 16
LOG2E = 1.4426950408889634
GELU_A = 0.7978845608028654
GELU_B = GELU_A * 0.044715

NN = (((1,), (0,)), ((), ()))
NT = (((1,), (1,)), ((), ()))
TN = (((0,), (0,)), ((), ()))


def dot(left, right, dims):
    return lax.dot_general(left, right, dims, preferred_element_type=single)


def params(vmem=56 << 20):
    return pltpu.CompilerParams(vmem_limit_bytes=vmem)


def cost(flops, moved):
    return pl.CostEstimate(flops=1024, bytes_accessed=1024, transcendentals=0)


def resident(shape):
    zeros = (0,) * len(shape)
    return pl.BlockSpec(shape, lambda *_: zeros, pipeline_mode=pl.Buffered(1))


def kept(shape):
    zeros = (0,) * len(shape)
    return pl.BlockSpec(shape, lambda *_: zeros)


def of_short(shape, half):
    tail = (0,) * (len(shape) - 1)
    return pl.BlockSpec(shape, lambda i: (jnp.minimum(i, half - 1),) + tail)


def of_long(shape, half):
    tail = (0,) * (len(shape) - 1)
    return pl.BlockSpec(shape, lambda i: (jnp.maximum(i - half, 0),) + tail)


def by_step(shape):
    tail = (0,) * (len(shape) - 1)
    return pl.BlockSpec(shape, lambda i: (i,) + tail)


def on_scalars():
    return pl.BlockSpec(memory_space=pltpu.SMEM)


def assemble(place, pieces, out_ref):
    columns = out_ref.shape[1]
    for i, piece in enumerate(pieces):
        rows = piece.shape[0]
        at = pl.multiple_of((place ^ i) * rows, rows)
        out_ref[pl.ds(at, rows), :] = piece[:, :columns]


def assemble_lines(place, pieces, out_ref):
    for piece, low in zip(pieces, (0, 2, 1, 3)):
        rows = piece.shape[1]
        for z in range(piece.shape[0]):
            at = pl.multiple_of((place ^ (z << 2 | low)) * rows, rows)
            out_ref[pl.ds(at, rows), :] = piece[z]


def standardize(rows):
    centre = rows - jnp.mean(rows, axis=-1, keepdims=True)
    factor = lax.rsqrt(jnp.mean(centre * centre, axis=-1, keepdims=True) + 1e-05)
    return centre * factor, factor


def norm_back(upper, scaled, factor, gain):
    inner = upper * gain
    return factor * (
        inner
        - jnp.mean(inner, axis=-1, keepdims=True)
        - scaled * jnp.mean(inner * scaled, axis=-1, keepdims=True)
    )


def start_rows(step, half, size, short_ref, long_ref, embed_ref, emit):
    def group(rows_ref, length, number, is_short):
        rows = rows_ref[...].astype(single)
        parts = []
        for s in range(size // length):
            embed = embed_ref[pl.ds(number + s, 1), :]
            parts.append(rows[s * length : (s + 1) * length] + embed)
        emit(parts[0] if len(parts) == 1 else jnp.concatenate(parts, axis=0), is_short)

    @pl.when(step < half)
    def _():
        group(short_ref, SHORT, step * (size // SHORT), True)

    @pl.when(step >= half)
    def _():
        group(long_ref, LONG, half * (size // SHORT) + (step - half) * (size // LONG), False)


def apart(pair):
    first_half = lax.broadcasted_iota(jnp.int32, (1, PAIR), 1) < HEAD_DIM
    zeros = jnp.zeros_like(pair)
    return jnp.concatenate([jnp.where(first_half, pair, zeros), jnp.where(first_half, zeros, pair)], axis=0)


def apart_turned(pair):
    turned = pair.T
    upper = lax.broadcasted_iota(jnp.int32, (PAIR, 1), 0) < HEAD_DIM
    zeros = jnp.zeros_like(turned)
    return jnp.concatenate([jnp.where(upper, turned, zeros), jnp.where(upper, zeros, turned)], axis=1)


def own_half(both):
    length = both.shape[0] // 2
    first_half = lax.broadcasted_iota(jnp.int32, (1, PAIR), 1) < HEAD_DIM
    return jnp.where(first_half, both[:length], both[length:])


def attend(query, keys, values, probs_ref, at):
    length = query.shape[0]
    scores = dot(apart(keys), query, NT)
    parts = []
    for j in range(2):
        own = scores[j * length : (j + 1) * length]
        summit = jnp.max(own, axis=0, keepdims=True)
        expo = jnp.exp2((own - summit) * (LOG2E * HEAD_DIM ** (-0.5)))
        total = jnp.sum(expo, axis=0, keepdims=True)
        parts.append((expo * (1.0 / total)).astype(bfloat))
    probs = jnp.concatenate(parts, axis=0)
    probs_ref[at] = probs
    return dot(apart_turned(values), probs, NN).T


def forward_attention(
    half, width, n_pieces, place_ref, short_ref, long_ref, embed_ref, small_ref, *refs
):
    pieces = refs[:n_pieces]
    first_ref, qkv_ref, probs_short, probs_long, mixed_ref, weight, joined = refs[n_pieces:]
    step = pl.program_id(0)
    heads = width // HEAD_DIM

    @pl.when(step == 0)
    def _():
        place = place_ref[0]
        assemble(place, pieces, weight)
        joined[...] = jnp.zeros_like(joined)
        joined[:, 0:width] = small_ref[2:3]
        joined[:, 2 * width :] = small_ref[3:4]

    def emit(start, is_short):
        scaled, _ = standardize(start)
        first = (scaled * small_ref[0:1, :] + small_ref[1:2, :]).astype(bfloat)
        first_ref[...] = first
        for part in range(3):
            cols = slice(part * width, (part + 1) * width)
            qkv_ref[:, cols] = (dot(first, weight[:, cols], NN) + joined[:, cols]).astype(bfloat)
        length = 128 if is_short else TILE
        probs_ref = probs_short if is_short else probs_long
        for s in range(TILE // length):
            rows = slice(s * length, (s + 1) * length)
            for pair in range(heads // 2):
                cols = slice(pair * PAIR, (pair + 1) * PAIR)
                query = qkv_ref[rows, cols]
                keys = qkv_ref[rows, width + pair * PAIR : width + (pair + 1) * PAIR]
                values = qkv_ref[rows, 2 * width + pair * PAIR : 2 * width + (pair + 1) * PAIR]
                mixed_ref[rows, cols] = attend(query, keys, values, probs_ref, (s, pair)).astype(
                    bfloat
                )

    start_rows(step, half, short_ref.shape[0], short_ref, long_ref, embed_ref, emit)


def forward_up(
    half, width, hidden, n_up, place_ref, short_ref, long_ref, embed_ref, small_ref, bias_ref, mixed_ref, *refs
):
    ups = refs[:n_up]
    middle_ref, second_ref, active_ref, slope_ref, weight = refs[n_up:]
    step = pl.program_id(0)

    @pl.when(step == 0)
    def _():
        assemble_lines(place_ref[0], ups, weight)

    def emit(start, _):
        middle_ref[...] = start

    start_rows(step, half, short_ref.shape[0], short_ref, long_ref, embed_ref, emit)
    middle = middle_ref[...] + dot(mixed_ref[...], weight[:, :width], NN) + small_ref[4:5, :]
    middle_ref[...] = middle
    scaled, _ = standardize(middle)
    second = (scaled * small_ref[5:6, :] + small_ref[6:7, :]).astype(bfloat)
    second_ref[...] = second
    for at in range(0, hidden, width):
        cols = slice(at, at + width)
        u = dot(second, weight[:, width + at : 2 * width + at], NN) + bias_ref[:, cols]
        square = u * u
        half_up = 0.5 + 0.5 * jnp.tanh(u * (GELU_A + GELU_B * square))
        active = u * half_up
        active_ref[:, cols] = active.astype(bfloat)
        slope = half_up + active * (1.0 - half_up) * (2.0 * GELU_A + 6.0 * GELU_B * square)
        slope_ref[:, cols] = slope.astype(bfloat)


def store_shard(place, shard, value, keep_ref, send_ref):
    rel = place ^ shard
    slot = ((rel >> 1) & 1) * 4 + (rel >> 2)

    @pl.when((rel & 1) == 0)
    def _():
        keep_ref[slot] = value

    @pl.when((rel & 1) == 1)
    def _():
        send_ref[slot] = value


def down_weight_back(active_ref, short_ref, long_ref, out_ref, grad):
    @pl.when(pl.program_id(0) == 0)
    def _():
        split = short_ref.shape[0]
        grad[:split, :] = short_ref[...]
        grad[split:, :] = long_ref[...]

    out_ref[...] = dot(active_ref[...], grad[...], TN).astype(bfloat)


def weight_back(parts, place_ref, *refs):
    lefts, rights = refs[: len(parts)], refs[len(parts) : 2 * len(parts)]
    keep_ref, send_ref, turned = refs[2 * len(parts) :]
    step = pl.program_id(0)
    place = place_ref[0]
    rows = keep_ref.shape[1]
    begin = 0
    for left_ref, right_ref, tiles in zip(lefts, rights, parts):

        @pl.when(step == begin)
        def _(left_ref=left_ref):
            turned[...] = left_ref[...].T

        def work(right_ref=right_ref):
            total = dot(turned[...], right_ref[...], NN).astype(bfloat)
            for k in range(SHARDS):
                store_shard(place, k, total[k * rows : (k + 1) * rows], keep_ref, send_ref)

        if len(parts) == 1:
            work()
        else:
            pl.when(jnp.logical_and(step >= begin, step < begin + tiles))(work)
        begin += tiles


def feed_back(
    half, width, hidden, n, place_ref, short_ref, long_ref, slope_ref, middle_ref, small_ref, *refs
):
    ups, downs = refs[:n], refs[n : 2 * n]
    (hidden_grad_ref, branch_ref, middle_grad_ref, mixed_grad_ref, vector_ref, bias_ref, weight, down, grad) = refs[
        2 * n :
    ]
    step = pl.program_id(0)

    @pl.when(step == 0)
    def _():
        assemble_lines(place_ref[0], ups, weight)
        assemble_lines(place_ref[0], downs, down)
        vector_ref[...] = jnp.zeros_like(vector_ref)
        bias_ref[...] = jnp.zeros_like(bias_ref)

    @pl.when(step < half)
    def _():
        grad[...] = short_ref[...]

    @pl.when(step >= half)
    def _():
        grad[...] = long_ref[...]

    upper = jnp.zeros((grad.shape[0], width), single)
    for at in range(0, hidden, width):
        cols = slice(at, at + width)
        passed = dot(grad[...], down[cols, :], NT) * slope_ref[:, cols].astype(single)
        low = passed.astype(bfloat)
        hidden_grad_ref[:, cols] = low
        bias_ref[:, cols] += jnp.sum(low.astype(single), axis=0, keepdims=True)
        upper += dot(low, weight[:, width + at : 2 * width + at], NT)
    scaled, factor = standardize(middle_ref[...])
    rows = grad[...].astype(single)
    middle_grad = rows + norm_back(upper, scaled, factor, small_ref[5:6, :])
    middle_grad_ref[...] = middle_grad
    branch = middle_grad.astype(bfloat)
    branch_ref[...] = branch
    mixed_grad_ref[...] = dot(branch, weight[:, :width], NT).astype(bfloat)
    vector_ref[0:1, :] += jnp.sum(upper * scaled, axis=0, keepdims=True)
    vector_ref[1:2, :] += jnp.sum(upper, axis=0, keepdims=True)
    vector_ref[2:3, :] += jnp.sum(branch.astype(single), axis=0, keepdims=True)
    vector_ref[3:4, :] += jnp.sum(rows, axis=0, keepdims=True)


def attend_back(query, keys, values, upper, probs):
    length = query.shape[0]
    probs_grad = dot(apart(values), upper, NT)
    parts = []
    for j in range(2):
        rows = slice(j * length, (j + 1) * length)
        wide, own = probs[rows].astype(single), probs_grad[rows]
        inner = jnp.sum(wide * own, axis=0, keepdims=True)
        parts.append((wide * (own - inner)).astype(bfloat))
    scores_grad = jnp.concatenate(parts, axis=0)
    scale = HEAD_DIM ** (-0.5)
    query_grad = dot(apart_turned(keys), scores_grad, NN).T * scale
    keys_grad = own_half(dot(scores_grad, query, NN)) * scale
    values_grad = own_half(dot(probs, upper, NN))
    return query_grad.astype(bfloat), keys_grad.astype(bfloat), values_grad.astype(bfloat)


def backward_attention(half, width, qkv_ref, mixed_grad_ref, probs_short, probs_long, grad_ref):
    step = pl.program_id(0)
    heads = width // HEAD_DIM

    def group(length, probs_ref):
        for s in range(TILE // length):
            rows = slice(s * length, (s + 1) * length)
            for pair in range(heads // 2):
                spots = [slice(part * width + pair * PAIR, part * width + (pair + 1) * PAIR) for part in range(3)]
                query, keys, values = (qkv_ref[rows, spot] for spot in spots)
                upper = mixed_grad_ref[rows, spots[0]]
                for spot, value in zip(spots, attend_back(query, keys, values, upper, probs_ref[s, pair])):
                    grad_ref[rows, spot] = value

    pl.when(step < half)(lambda: group(128, probs_short))
    pl.when(step >= half)(lambda: group(TILE, probs_long))


def start_back(
    half, width, n_first, place_ref, short_ref, long_ref, embed_ref, small_ref, middle_grad_ref, grad_ref, *refs
):
    firsts = refs[:n_first]
    in_short, in_long, vector_ref, sums_ref, weight = refs[n_first:]
    step = pl.program_id(0)
    size = short_ref.shape[0]

    @pl.when(step == 0)
    def _():
        assemble(place_ref[0], firsts, weight)
        vector_ref[...] = jnp.zeros_like(vector_ref)
        sums_ref[...] = jnp.zeros_like(sums_ref)

    def emit(start, is_short):
        upper = dot(grad_ref[...], weight[...], NT)
        scaled, factor = standardize(start)
        start_grad = middle_grad_ref[...] + norm_back(upper, scaled, factor, small_ref[0:1, :])
        vector_ref[0:1, :] += jnp.sum(upper * scaled, axis=0, keepdims=True)
        vector_ref[1:2, :] += jnp.sum(upper, axis=0, keepdims=True)
        vector_ref[2:3, :] += jnp.sum(grad_ref[:, :width].astype(single), axis=0, keepdims=True)
        vector_ref[3:4, :] += jnp.sum(grad_ref[:, 2 * width :].astype(single), axis=0, keepdims=True)
        out, length = (in_short, SHORT) if is_short else (in_long, LONG)
        out[...] = start_grad.astype(bfloat)
        number = step * (size // SHORT) if is_short else half * (size // SHORT) + (step - half) * (size // LONG)
        for s in range(size // length):
            sums_ref[pl.ds(number + s, 1), :] = jnp.sum(
                start_grad[s * length : (s + 1) * length], axis=0, keepdims=True
            )

    start_rows(step, half, short_ref.shape[0], short_ref, long_ref, embed_ref, emit)


def forward_down(half, n, place_ref, middle_ref, active_ref, small_ref, *refs):
    downs, (out_short, out_long, down) = refs[:n], refs[n:]
    step = pl.program_id(0)

    @pl.when(step == 0)
    def _():
        assemble_lines(place_ref[0], downs, down)

    result = middle_ref[...] + dot(active_ref[...], down[...], NN) + small_ref[7:8, :]

    @pl.when(step < half)
    def _():
        out_short[...] = result.astype(bfloat)

    @pl.when(step >= half)
    def _():
        out_long[...] = result.astype(bfloat)


def flip(bit):
    return [(i, i ^ bit) for i in range(SHARDS)]


def across(array, bit):
    return lax.ppermute(array, "fsdp", flip(bit))


def to_replica(array):
    return lax.ppermute(array, "rep", [(0, 1), (1, 0)])


def tie(*values):
    return lax.optimization_barrier(values)


def spread(line, other):
    others = [other] + [across(piece, 2) for piece in line[1:]]
    pieces = []
    for held in zip(line, others):
        for piece in held:
            pieces += [piece, across(piece, 1)]
    return pieces


def along(shard):
    return [shard] + [across(shard, z << 2) for z in (1, 2, 3)]


def added(*terms):
    total = terms[0].astype(single)
    for term in terms[1:]:
        total = total + term.astype(single)
    return total


class Scatter:
    def __init__(self, count, keep, send):
        self.count = count
        self.keep = keep
        if count == SHARDS:
            self.came = across(send, 1)
        else:
            both = jnp.stack([keep, send]).reshape((2, 2, 4) + keep.shape[1:])
            whole = both.transpose(2, 1, 0, 3, 4).reshape(-1, keep.shape[2])
            self.share = lax.psum_scatter(whole, "fsdp", scatter_dimension=0, tiled=True)

    def over_y(self, *after):
        if self.count != SHARDS:
            return after
        self.keep, self.came, after = tie(self.keep, self.came, after)
        theirs = added(self.keep[4:], self.came[4:]).astype(bfloat)
        self.keep = added(self.keep[:4], self.came[:4]).astype(bfloat)
        theirs, after = tie(theirs, after)
        self.came = across(theirs, 2)
        return after

    def over_z(self, *after):
        if self.count != SHARDS:
            return after
        self.keep, self.came, after = tie(self.keep, self.came, after)
        slots = [added(self.keep[z], self.came[z]) for z in range(4)]
        self.keep = slots[0].astype(bfloat)
        lows, after = tie([slot.astype(bfloat) for slot in slots[1:]], after)
        self.came = [across(low, (z + 1) << 2) for z, low in enumerate(lows)]
        return after

    def over_x(self, *after):
        if self.count == SHARDS:
            terms, after = tie([self.keep] + self.came, after)
            self.share = added(*terms).astype(bfloat)
        else:
            self.share = self.share.astype(bfloat)
        self.share, after = tie(self.share, after)
        self.other = to_replica(self.share)
        return after

    def result(self):
        return added(self.share, self.other)


def shards(
    count,
    input_short,
    input_long,
    steps_short,
    steps_long,
    upstream_short,
    upstream_long,
    step_table,
    attn_gain,
    attn_shift,
    qkv_weight,
    query_bias,
    value_bias,
    out_weight,
    out_bias,
    ffn_gain,
    ffn_shift,
    up_weight,
    up_bias,
    down_weight,
    down_bias,
):
    width, rows = out_weight.shape[1], out_weight.shape[0]
    hidden = up_weight.shape[1]
    n_short, n_long = steps_short.shape[0], steps_long.shape[0]
    short = input_short.reshape(-1, width)
    long = input_long.reshape(-1, width)
    up_short = upstream_short.reshape(-1, width)
    up_long = upstream_long.reshape(-1, width)
    total = short.shape[0] + long.shape[0]
    grid = total // TILE
    half = short.shape[0] // TILE
    heads = width // HEAD_DIM
    timesteps = step_table.shape[0]

    first_shard = qkv_weight.astype(bfloat)
    up_shard = jnp.concatenate([out_weight, up_weight], axis=1).astype(bfloat)
    down_shard = down_weight.astype(bfloat)

    place = (lax.axis_index("fsdp") if count == SHARDS else jnp.int32(0)).reshape(1).astype(jnp.int32)
    owners = width // rows
    steps = jnp.concatenate([steps_short, steps_long])
    marks = steps.shape[0]
    vectors = [attn_gain, attn_shift, query_bias, value_bias, out_bias, ffn_gain, ffn_shift, down_bias]
    own = jnp.concatenate(vectors + [up_bias]).astype(bfloat)
    told = lax.all_to_all(jnp.broadcast_to(steps, (owners, marks)), "fsdp", 0, 0, tiled=True)
    if count == SHARDS:
        shard_z = along(first_shard)
        shard_y = across(first_shard, 2)
        told, shard_z, shard_y = tie(told, shard_z, shard_y)
    chosen = (told.reshape(-1, 1) == jnp.arange(timesteps, dtype=jnp.int32)).astype(bfloat)
    chosen = jnp.dot(chosen, step_table.astype(bfloat), preferred_element_type=single).astype(bfloat)
    chosen = chosen.reshape(owners, marks * rows)
    chosen = jnp.concatenate([chosen, jnp.broadcast_to(own, (owners, own.shape[0]))], axis=1)
    told = lax.all_to_all(chosen, "fsdp", 0, 0, tiled=True)
    most = (marks + 8) * rows
    told = told.astype(single)
    rest = told[:, :most].reshape(owners, marks + 8, rows).transpose(1, 0, 2).reshape(marks + 8, width)
    embed = jnp.pad(rest[:marks], ((0, 8 - marks), (0, 0)))
    smalls = rest[marks:]
    bias = told[:, most:].reshape(1, hidden)
    if count == SHARDS:
        up_shard, shard_y = tie(up_shard, shard_y)
        first_pieces = spread(shard_z, shard_y)
        up_line, others, embed, smalls, bias = tie(
            along(up_shard), [first_pieces[i] for i in (6, 10, 14)], embed, smalls, bias
        )
        first_pieces[6], first_pieces[10], first_pieces[14] = others
        up_line = jnp.stack(up_line)
        up_line, down_shard, first_pieces[-1] = tie(up_line, down_shard, first_pieces[-1])
        up_core, up_other = across(up_line, 1), across(up_line, 2)
        down_line = along(down_shard)
    else:
        first_pieces = [lax.all_gather(first_shard, "fsdp", axis=0, tiled=True)]
        up_pieces = [lax.all_gather(up_shard, "fsdp", axis=0, tiled=True)[None]]
        down_pieces = [lax.all_gather(down_shard, "fsdp", axis=0, tiled=True)[None]]
    n = len(first_pieces)
    first_specs = [resident(p.shape) for p in first_pieces]

    tile = (TILE, width)
    short_spec, long_spec = of_short(tile, half), of_long(tile, half)
    band, half_band = (BAND, width), short.shape[0] // BAND
    short_band, long_band = of_short(band, half_band), of_long(band, half_band)
    probs_short_spec = of_short((TILE // SHORT, heads // 2, 2 * SHORT, SHORT), half)
    probs_long_spec = of_long((1, heads // 2, 2 * LONG, LONG), half)
    shape = jax.ShapeDtypeStruct
    first, qkv, probs_short, probs_long, mixed = pl.pallas_call(
        functools.partial(forward_attention, half, width, n),
        grid=(grid,),
        in_specs=[on_scalars(), short_spec, long_spec, kept((8, width)), kept((8, width))] + first_specs,
        out_specs=[
            by_step(tile),
            by_step((TILE, 3 * width)),
            probs_short_spec,
            probs_long_spec,
            by_step(tile),
        ],
        out_shape=[
            shape((total, width), bfloat),
            shape((total, 3 * width), bfloat),
            shape((n_short, heads // 2, 2 * SHORT, SHORT), bfloat),
            shape((n_long, heads // 2, 2 * LONG, LONG), bfloat),
            shape((total, width), bfloat),
        ],
        scratch_shapes=[pltpu.VMEM((width, 3 * width), bfloat), pltpu.VMEM((1, 3 * width), single)],
        compiler_params=params(),
        cost_estimate=cost(2 * total * width * 3 * width * 2, total * width * 40),
        name="forward_attention",
    )(place, short, long, embed, smalls, *first_pieces)

    owners = width // rows
    if count == SHARDS:
        down_line, up_other, up_core, mixed = tie(down_line, up_other, up_core, mixed)
        up_pieces = [up_line, up_other, up_core, across(up_other, 1)]
        down_line = jnp.stack(down_line)
        down_line, up_pieces = tie(down_line, up_pieces)
        down_core, down_other = across(down_line, 1), across(down_line, 2)
    middle, second, active, slope = pl.pallas_call(
        functools.partial(forward_up, half_band, width, hidden, len(up_pieces)),
        grid=(total // BAND,),
        in_specs=[
            on_scalars(),
            short_band,
            long_band,
            kept((8, width)),
            kept((8, width)),
            kept((1, hidden)),
            by_step(band),
        ]
        + [resident(p.shape) for p in up_pieces],
        out_specs=[
            by_step(band),
            by_step(band),
            by_step((BAND, hidden)),
            by_step((BAND, hidden)),
        ],
        out_shape=[
            shape((total, width), single),
            shape((total, width), bfloat),
            shape((total, hidden), bfloat),
            shape((total, hidden), bfloat),
        ],
        scratch_shapes=[pltpu.VMEM((width, width + hidden), bfloat)],
        compiler_params=params(),
        cost_estimate=cost(2 * total * width * (width + hidden) * 2, total * width * 20),
        name="forward_up",
    )(place, short, long, embed, smalls, bias, mixed, *up_pieces)

    slots = SHARDS // 2
    whole_rows = width // SHARDS
    down_terms = pl.pallas_call(
        down_weight_back,
        grid=(hidden // width,),
        in_specs=[
            pl.BlockSpec((total, width), lambda i: (0, i)),
            kept(up_short.shape),
            kept(up_long.shape),
        ],
        out_specs=by_step((width, width)),
        out_shape=shape((hidden, width), bfloat),
        scratch_shapes=[pltpu.VMEM((total, width), bfloat)],
        compiler_params=params(),
        cost_estimate=cost(2 * total * width * hidden, total * width * 12),
        name="down_weight_back",
    )(active, up_short, up_long)
    down_share = lax.psum_scatter(down_terms, "fsdp", scatter_dimension=0, tiled=True)
    if count == SHARDS:
        down_terms, slope, down_other = tie(down_terms, slope, down_other)
        down_pieces = [down_line, down_other, down_core, across(down_other, 1)]

    hidden_grad, branch, middle_grad, mixed_grad, vectors, bias_grad = pl.pallas_call(
        functools.partial(feed_back, half_band, width, hidden, len(down_pieces)),
        grid=(total // BAND,),
        in_specs=[
            on_scalars(),
            short_band,
            long_band,
            by_step((BAND, hidden)),
            by_step(band),
            kept((8, width)),
        ]
        + [resident(p.shape) for p in [*up_pieces, *down_pieces]],
        out_specs=[
            by_step((BAND, hidden)),
            by_step(band),
            by_step(band),
            by_step(band),
            kept((8, width)),
            kept((1, hidden)),
        ],
        out_shape=[
            shape((total, hidden), bfloat),
            shape((total, width), bfloat),
            shape((total, width), single),
            shape((total, width), bfloat),
            shape((8, width), single),
            shape((1, hidden), single),
        ],
        scratch_shapes=[
            pltpu.VMEM((width, width + hidden), bfloat),
            pltpu.VMEM((hidden, width), bfloat),
            pltpu.VMEM(band, bfloat),
        ],
        compiler_params=params(),
        cost_estimate=cost(2 * total * width * (width + 2 * hidden), total * width * 30),
        name="feed_back",
    )(place, up_short, up_long, slope, middle, smalls, *up_pieces, *down_pieces)

    tiles = hidden // width
    column = lambda last: pl.BlockSpec((total, width), lambda i: (0, jnp.minimum(i, last)))
    out_block = pl.BlockSpec((slots, whole_rows, width), lambda i: (0, 0, i))
    up_keep, up_send = pl.pallas_call(
        functools.partial(weight_back, (1, tiles)),
        grid=(tiles + 1,),
        in_specs=[
            on_scalars(),
            kept((total, width)),
            kept((total, width)),
            kept((total, width)),
            pl.BlockSpec((total, width), lambda i: (0, jnp.maximum(i - 1, 0))),
        ],
        out_specs=[out_block] * 2,
        out_shape=[shape((slots, whole_rows, width + hidden), bfloat)] * 2,
        scratch_shapes=[pltpu.VMEM((width, total), bfloat)],
        compiler_params=params(),
        cost_estimate=cost(2 * total * width * (width + hidden), total * width * 20),
        name="up_weight_back",
    )(place, mixed, second, branch, hidden_grad)
    up_sum = Scatter(count, up_keep, up_send)
    (qkv,) = up_sum.over_y(qkv)

    projected_grad = pl.pallas_call(
        functools.partial(backward_attention, half, width),
        grid=(grid,),
        in_specs=[by_step((TILE, 3 * width)), by_step(tile), probs_short_spec, probs_long_spec],
        out_specs=by_step((TILE, 3 * width)),
        out_shape=shape((total, 3 * width), bfloat),
        compiler_params=params(),
        cost_estimate=cost(2 * total * width * 3 * width * 2, total * width * 20),
        name="backward_attention",
    )(qkv, mixed_grad, probs_short, probs_long)

    qkv_keep, qkv_send = pl.pallas_call(
        functools.partial(weight_back, (3,)),
        grid=(3,),
        in_specs=[on_scalars(), kept((total, width)), column(2)],
        out_specs=[out_block] * 2,
        out_shape=[shape((slots, whole_rows, 3 * width), bfloat)] * 2,
        scratch_shapes=[pltpu.VMEM((width, total), bfloat)],
        compiler_params=params(),
        cost_estimate=cost(2 * total * width * 3 * width, total * width * 16),
        name="qkv_weight_back",
    )(place, first, projected_grad)
    qkv_sum = Scatter(count, qkv_keep, qkv_send)
    middle_grad, qkv_sum.keep, down_share = up_sum.over_z(middle_grad, qkv_sum.keep, down_share)
    (middle_grad,) = qkv_sum.over_y(middle_grad)

    grad_short, grad_long, last_vectors, sums = pl.pallas_call(
        functools.partial(start_back, half_band, width, n),
        grid=(total // BAND,),
        in_specs=[
            on_scalars(),
            short_band,
            long_band,
            kept((8, width)),
            kept((8, width)),
            by_step(band),
            by_step((BAND, 3 * width)),
        ]
        + first_specs,
        out_specs=[short_band, long_band, kept((8, width)), kept((8, width))],
        out_shape=[
            shape(short.shape, bfloat),
            shape(long.shape, bfloat),
            shape((8, width), single),
            shape((8, width), single),
        ],
        scratch_shapes=[pltpu.VMEM((width, 3 * width), bfloat)],
        compiler_params=params(),
        cost_estimate=cost(2 * total * width * 3 * width, total * width * 30),
        name="start_back",
    )(place, short, long, embed, smalls, middle_grad, projected_grad, *first_pieces)
    owners = width // rows
    both = jnp.concatenate([vectors[:4], last_vectors[:4], sums[:marks]], axis=0)
    lines = both.shape[0]
    packed = both.reshape(lines, owners, rows).transpose(1, 0, 2).reshape(owners, lines * rows)
    own_steps = jnp.broadcast_to(steps.astype(single), (owners, marks))
    packed = jnp.concatenate([packed, bias_grad.reshape(owners, -1), own_steps], axis=1)
    packed = jnp.concatenate([packed, packed], axis=0)
    came = lax.all_to_all(packed, ("rep", "fsdp"), 0, 0, tiled=True)
    if count == SHARDS:
        up_sum.came, qkv_sum.came, middle, came = tie(up_sum.came, qkv_sum.came, middle, came)
    middle, down_share = up_sum.over_x(middle, down_share)
    down_other = to_replica(down_share)
    (middle,) = qkv_sum.over_z(middle)
    output_short, output_long = pl.pallas_call(
        functools.partial(forward_down, half_band, len(down_pieces)),
        grid=(total // BAND,),
        in_specs=[on_scalars(), by_step(band), by_step((BAND, hidden)), kept((8, width))]
        + [resident(p.shape) for p in down_pieces],
        out_specs=[short_band, long_band],
        out_shape=[shape(short.shape, bfloat), shape(long.shape, bfloat)],
        scratch_shapes=[pltpu.VMEM((hidden, width), bfloat)],
        compiler_params=params(),
        cost_estimate=cost(2 * total * width * hidden, total * width * 30),
        name="forward_down",
    )(place, middle, active, smalls, *down_pieces)

    vector_sums = jnp.sum(came[:, : 8 * rows], axis=0).reshape(8, rows)
    ends = lines * rows + hidden // owners
    up_bias_grad = jnp.sum(came[:, lines * rows : ends], axis=0)
    sequence_sums = came[:, 8 * rows : lines * rows].reshape(-1, rows)
    all_steps = came[:, ends:].astype(jnp.int32).reshape(-1)
    selector = (all_steps[:, None] == jnp.arange(timesteps, dtype=jnp.int32)[None, :]).astype(single)
    table_grad = lax.dot_general(
        selector,
        sequence_sums,
        TN,
        precision=lax.Precision.HIGHEST,
        preferred_element_type=single,
    )
    down_other, up_sum.other = qkv_sum.over_x(down_other, up_sum.other)
    up_grads, qkv_weight_grad = up_sum.result(), qkv_sum.result()
    down_weight_grad = added(down_share, down_other)
    return (
        output_short.reshape(input_short.shape),
        output_long.reshape(input_long.shape),
        grad_short.reshape(input_short.shape),
        grad_long.reshape(input_long.shape),
        table_grad,
        vector_sums[4],
        vector_sums[5],
        qkv_weight_grad,
        vector_sums[6],
        vector_sums[7],
        up_grads[:, :width],
        vector_sums[2],
        vector_sums[0],
        vector_sums[1],
        up_grads[:, width:],
        up_bias_grad,
        down_weight_grad,
        vector_sums[3],
    )


def solution(mesh):
    rows = P(("rep", "fsdp"), None, None)
    steps = P(("rep", "fsdp"))
    vector, matrix, table = P("fsdp"), P("fsdp", None), P(None, "fsdp")
    weights = (
        table,
        vector,
        vector,
        matrix,
        vector,
        vector,
        matrix,
        vector,
        vector,
        vector,
        matrix,
        vector,
        matrix,
        vector,
    )
    return jax.shard_map(
        functools.partial(shards, mesh.shape["fsdp"]),
        mesh=mesh,
        in_specs=(rows, rows, steps, steps, rows, rows) + weights,
        out_specs=(rows,) * 4 + weights,
        check_vma=False,
    )
```

```python
import functools

import jax
import jax.numpy as jnp
from jax import lax
from jax.experimental import pallas as pl
from jax.experimental.pallas import tpu as pltpu
from jax.sharding import PartitionSpec as P

bfloat = jnp.bfloat16
single = jnp.float32

HEAD_DIM = 64
PAIR = 2 * HEAD_DIM
TILE = 256
BAND = 256
SHORT = 128
LONG = 256
SHARDS = 16
LOG2E = 1.4426950408889634
GELU_A = 0.7978845608028654
GELU_B = GELU_A * 0.044715

NN = (((1,), (0,)), ((), ()))
NT = (((1,), (1,)), ((), ()))
TN = (((0,), (0,)), ((), ()))


def dot(left, right, dims):
    return lax.dot_general(left, right, dims, preferred_element_type=single)


def params(vmem=56 << 20):
    return pltpu.CompilerParams(vmem_limit_bytes=vmem)


def cost(flops, moved):
    return pl.CostEstimate(flops=1024, bytes_accessed=1024, transcendentals=0)


def resident(shape):
    zeros = (0,) * len(shape)
    return pl.BlockSpec(shape, lambda *_: zeros, pipeline_mode=pl.Buffered(1))


def kept(shape):
    zeros = (0,) * len(shape)
    return pl.BlockSpec(shape, lambda *_: zeros)


def of_short(shape, half):
    tail = (0,) * (len(shape) - 1)
    return pl.BlockSpec(shape, lambda i: (jnp.minimum(i, half - 1),) + tail)


def of_long(shape, half):
    tail = (0,) * (len(shape) - 1)
    return pl.BlockSpec(shape, lambda i: (jnp.maximum(i - half, 0),) + tail)


def by_step(shape):
    tail = (0,) * (len(shape) - 1)
    return pl.BlockSpec(shape, lambda i: (i,) + tail)


def on_scalars():
    return pl.BlockSpec(memory_space=pltpu.SMEM)


def assemble(place, pieces, out_ref):
    columns = out_ref.shape[1]
    for i, piece in enumerate(pieces):
        rows = piece.shape[0]
        at = pl.multiple_of((place ^ i) * rows, rows)
        out_ref[pl.ds(at, rows), :] = piece[:, :columns]


def assemble_lines(place, pieces, out_ref):
    for piece, low in zip(pieces, (0, 2, 1, 3)):
        rows = piece.shape[1]
        for z in range(piece.shape[0]):
            at = pl.multiple_of((place ^ (z << 2 | low)) * rows, rows)
            out_ref[pl.ds(at, rows), :] = piece[z]


def standardize(rows):
    centre = rows - jnp.mean(rows, axis=-1, keepdims=True)
    factor = lax.rsqrt(jnp.mean(centre * centre, axis=-1, keepdims=True) + 1e-05)
    return centre * factor, factor


def norm_back(upper, scaled, factor, gain):
    inner = upper * gain
    return factor * (
        inner
        - jnp.mean(inner, axis=-1, keepdims=True)
        - scaled * jnp.mean(inner * scaled, axis=-1, keepdims=True)
    )


def start_rows(step, half, size, short_ref, long_ref, embed_ref, emit):
    def group(rows_ref, length, number, is_short):
        rows = rows_ref[...].astype(single)
        parts = []
        for s in range(size // length):
            embed = embed_ref[pl.ds(number + s, 1), :]
            parts.append(rows[s * length : (s + 1) * length] + embed)
        emit(parts[0] if len(parts) == 1 else jnp.concatenate(parts, axis=0), is_short)

    @pl.when(step < half)
    def _():
        group(short_ref, SHORT, step * (size // SHORT), True)

    @pl.when(step >= half)
    def _():
        group(long_ref, LONG, half * (size // SHORT) + (step - half) * (size // LONG), False)


def apart(pair):
    first_half = lax.broadcasted_iota(jnp.int32, (1, PAIR), 1) < HEAD_DIM
    zeros = jnp.zeros_like(pair)
    return jnp.concatenate([jnp.where(first_half, pair, zeros), jnp.where(first_half, zeros, pair)], axis=0)


def apart_turned(pair):
    turned = pair.T
    upper = lax.broadcasted_iota(jnp.int32, (PAIR, 1), 0) < HEAD_DIM
    zeros = jnp.zeros_like(turned)
    return jnp.concatenate([jnp.where(upper, turned, zeros), jnp.where(upper, zeros, turned)], axis=1)


def own_half(both):
    length = both.shape[0] // 2
    first_half = lax.broadcasted_iota(jnp.int32, (1, PAIR), 1) < HEAD_DIM
    return jnp.where(first_half, both[:length], both[length:])


def attend(query, keys, values, probs_ref, at):
    length = query.shape[0]
    scores = dot(apart(keys), query, NT)
    parts = []
    for j in range(2):
        own = scores[j * length : (j + 1) * length]
        summit = jnp.max(own, axis=0, keepdims=True)
        expo = jnp.exp2((own - summit) * (LOG2E * HEAD_DIM ** (-0.5)))
        total = jnp.sum(expo, axis=0, keepdims=True)
        parts.append((expo * (1.0 / total)).astype(bfloat))
    probs = jnp.concatenate(parts, axis=0)
    probs_ref[at] = probs
    return dot(apart_turned(values), probs, NN).T


def forward_attention(
    half, width, n_pieces, place_ref, short_ref, long_ref, embed_ref, small_ref, *refs
):
    pieces = refs[:n_pieces]
    first_ref, qkv_ref, probs_short, probs_long, mixed_ref, weight, joined = refs[n_pieces:]
    step = pl.program_id(0)
    heads = width // HEAD_DIM

    @pl.when(step == 0)
    def _():
        place = place_ref[0]
        assemble(place, pieces, weight)
        joined[...] = jnp.zeros_like(joined)
        joined[:, 0:width] = small_ref[2:3]
        joined[:, 2 * width :] = small_ref[3:4]

    def emit(start, is_short):
        scaled, _ = standardize(start)
        first = (scaled * small_ref[0:1, :] + small_ref[1:2, :]).astype(bfloat)
        first_ref[...] = first
        for part in range(3):
            cols = slice(part * width, (part + 1) * width)
            qkv_ref[:, cols] = (dot(first, weight[:, cols], NN) + joined[:, cols]).astype(bfloat)
        length = 128 if is_short else TILE
        probs_ref = probs_short if is_short else probs_long
        for s in range(TILE // length):
            rows = slice(s * length, (s + 1) * length)
            for pair in range(heads // 2):
                cols = slice(pair * PAIR, (pair + 1) * PAIR)
                query = qkv_ref[rows, cols]
                keys = qkv_ref[rows, width + pair * PAIR : width + (pair + 1) * PAIR]
                values = qkv_ref[rows, 2 * width + pair * PAIR : 2 * width + (pair + 1) * PAIR]
                mixed_ref[rows, cols] = attend(query, keys, values, probs_ref, (s, pair)).astype(
                    bfloat
                )

    start_rows(step, half, short_ref.shape[0], short_ref, long_ref, embed_ref, emit)


def forward_up(
    half, width, hidden, n_up, place_ref, short_ref, long_ref, embed_ref, small_ref, bias_ref, mixed_ref, *refs
):
    ups = refs[:n_up]
    middle_ref, second_ref, active_ref, slope_ref, weight = refs[n_up:]
    step = pl.program_id(0)

    @pl.when(step == 0)
    def _():
        assemble_lines(place_ref[0], ups, weight)

    def emit(start, _):
        middle_ref[...] = start

    start_rows(step, half, short_ref.shape[0], short_ref, long_ref, embed_ref, emit)
    middle = middle_ref[...] + dot(mixed_ref[...], weight[:, :width], NN) + small_ref[4:5, :]
    middle_ref[...] = middle
    scaled, _ = standardize(middle)
    second = (scaled * small_ref[5:6, :] + small_ref[6:7, :]).astype(bfloat)
    second_ref[...] = second
    for at in range(0, hidden, width):
        cols = slice(at, at + width)
        u = dot(second, weight[:, width + at : 2 * width + at], NN) + bias_ref[:, cols]
        square = u * u
        half_up = 0.5 + 0.5 * jnp.tanh(u * (GELU_A + GELU_B * square))
        active = u * half_up
        active_ref[:, cols] = active.astype(bfloat)
        slope = half_up + active * (1.0 - half_up) * (2.0 * GELU_A + 6.0 * GELU_B * square)
        slope_ref[:, cols] = slope.astype(bfloat)


def store_shard(place, shard, value, keep_ref, send_ref):
    rel = place ^ shard
    slot = ((rel >> 1) & 1) * 4 + (rel >> 2)

    @pl.when((rel & 1) == 0)
    def _():
        keep_ref[slot] = value

    @pl.when((rel & 1) == 1)
    def _():
        send_ref[slot] = value


def down_weight_back(active_ref, short_ref, long_ref, out_ref, grad):
    @pl.when(pl.program_id(0) == 0)
    def _():
        split = short_ref.shape[0]
        grad[:split, :] = short_ref[...]
        grad[split:, :] = long_ref[...]

    out_ref[...] = dot(active_ref[...], grad[...], TN).astype(bfloat)


def weight_back(parts, place_ref, *refs):
    lefts, rights = refs[: len(parts)], refs[len(parts) : 2 * len(parts)]
    keep_ref, send_ref, turned = refs[2 * len(parts) :]
    step = pl.program_id(0)
    place = place_ref[0]
    rows = keep_ref.shape[1]
    begin = 0
    for left_ref, right_ref, tiles in zip(lefts, rights, parts):

        @pl.when(step == begin)
        def _(left_ref=left_ref):
            turned[...] = left_ref[...].T

        def work(right_ref=right_ref):
            total = dot(turned[...], right_ref[...], NN).astype(bfloat)
            for k in range(SHARDS):
                store_shard(place, k, total[k * rows : (k + 1) * rows], keep_ref, send_ref)

        if len(parts) == 1:
            work()
        else:
            pl.when(jnp.logical_and(step >= begin, step < begin + tiles))(work)
        begin += tiles


def feed_back(
    half, width, hidden, n, place_ref, short_ref, long_ref, slope_ref, middle_ref, small_ref, *refs
):
    ups, downs = refs[:n], refs[n : 2 * n]
    (hidden_grad_ref, branch_ref, middle_grad_ref, mixed_grad_ref, vector_ref, bias_ref, weight, down, grad) = refs[
        2 * n :
    ]
    step = pl.program_id(0)

    @pl.when(step == 0)
    def _():
        assemble_lines(place_ref[0], ups, weight)
        assemble_lines(place_ref[0], downs, down)
        vector_ref[...] = jnp.zeros_like(vector_ref)
        bias_ref[...] = jnp.zeros_like(bias_ref)

    @pl.when(step < half)
    def _():
        grad[...] = short_ref[...]

    @pl.when(step >= half)
    def _():
        grad[...] = long_ref[...]

    upper = jnp.zeros((grad.shape[0], width), single)
    for at in range(0, hidden, width):
        cols = slice(at, at + width)
        passed = dot(grad[...], down[cols, :], NT) * slope_ref[:, cols].astype(single)
        low = passed.astype(bfloat)
        hidden_grad_ref[:, cols] = low
        bias_ref[:, cols] += jnp.sum(low.astype(single), axis=0, keepdims=True)
        upper += dot(low, weight[:, width + at : 2 * width + at], NT)
    scaled, factor = standardize(middle_ref[...])
    rows = grad[...].astype(single)
    middle_grad = rows + norm_back(upper, scaled, factor, small_ref[5:6, :])
    middle_grad_ref[...] = middle_grad
    branch = middle_grad.astype(bfloat)
    branch_ref[...] = branch
    mixed_grad_ref[...] = dot(branch, weight[:, :width], NT).astype(bfloat)
    vector_ref[0:1, :] += jnp.sum(upper * scaled, axis=0, keepdims=True)
    vector_ref[1:2, :] += jnp.sum(upper, axis=0, keepdims=True)
    vector_ref[2:3, :] += jnp.sum(branch.astype(single), axis=0, keepdims=True)
    vector_ref[3:4, :] += jnp.sum(rows, axis=0, keepdims=True)


def attend_back(query, keys, values, upper, probs):
    length = query.shape[0]
    probs_grad = dot(apart(values), upper, NT)
    parts = []
    for j in range(2):
        rows = slice(j * length, (j + 1) * length)
        wide, own = probs[rows].astype(single), probs_grad[rows]
        inner = jnp.sum(wide * own, axis=0, keepdims=True)
        parts.append((wide * (own - inner)).astype(bfloat))
    scores_grad = jnp.concatenate(parts, axis=0)
    scale = HEAD_DIM ** (-0.5)
    query_grad = dot(apart_turned(keys), scores_grad, NN).T * scale
    keys_grad = own_half(dot(scores_grad, query, NN)) * scale
    values_grad = own_half(dot(probs, upper, NN))
    return query_grad.astype(bfloat), keys_grad.astype(bfloat), values_grad.astype(bfloat)


def backward_attention(half, width, qkv_ref, mixed_grad_ref, probs_short, probs_long, grad_ref):
    step = pl.program_id(0)
    heads = width // HEAD_DIM

    def group(length, probs_ref):
        for s in range(TILE // length):
            rows = slice(s * length, (s + 1) * length)
            for pair in range(heads // 2):
                spots = [slice(part * width + pair * PAIR, part * width + (pair + 1) * PAIR) for part in range(3)]
                query, keys, values = (qkv_ref[rows, spot] for spot in spots)
                upper = mixed_grad_ref[rows, spots[0]]
                for spot, value in zip(spots, attend_back(query, keys, values, upper, probs_ref[s, pair])):
                    grad_ref[rows, spot] = value

    pl.when(step < half)(lambda: group(128, probs_short))
    pl.when(step >= half)(lambda: group(TILE, probs_long))


def start_back(
    half, width, n_first, place_ref, short_ref, long_ref, embed_ref, small_ref, middle_grad_ref, grad_ref, *refs
):
    firsts = refs[:n_first]
    in_short, in_long, vector_ref, sums_ref, weight = refs[n_first:]
    step = pl.program_id(0)
    size = short_ref.shape[0]

    @pl.when(step == 0)
    def _():
        assemble(place_ref[0], firsts, weight)
        vector_ref[...] = jnp.zeros_like(vector_ref)
        sums_ref[...] = jnp.zeros_like(sums_ref)

    def emit(start, is_short):
        upper = dot(grad_ref[...], weight[...], NT)
        scaled, factor = standardize(start)
        start_grad = middle_grad_ref[...] + norm_back(upper, scaled, factor, small_ref[0:1, :])
        vector_ref[0:1, :] += jnp.sum(upper * scaled, axis=0, keepdims=True)
        vector_ref[1:2, :] += jnp.sum(upper, axis=0, keepdims=True)
        vector_ref[2:3, :] += jnp.sum(grad_ref[:, :width].astype(single), axis=0, keepdims=True)
        vector_ref[3:4, :] += jnp.sum(grad_ref[:, 2 * width :].astype(single), axis=0, keepdims=True)
        out, length = (in_short, SHORT) if is_short else (in_long, LONG)
        out[...] = start_grad.astype(bfloat)
        number = step * (size // SHORT) if is_short else half * (size // SHORT) + (step - half) * (size // LONG)
        for s in range(size // length):
            sums_ref[pl.ds(number + s, 1), :] = jnp.sum(
                start_grad[s * length : (s + 1) * length], axis=0, keepdims=True
            )

    start_rows(step, half, short_ref.shape[0], short_ref, long_ref, embed_ref, emit)


def forward_down(half, n, place_ref, middle_ref, active_ref, small_ref, *refs):
    downs, (out_short, out_long, down) = refs[:n], refs[n:]
    step = pl.program_id(0)

    @pl.when(step == 0)
    def _():
        assemble_lines(place_ref[0], downs, down)

    result = middle_ref[...] + dot(active_ref[...], down[...], NN) + small_ref[7:8, :]

    @pl.when(step < half)
    def _():
        out_short[...] = result.astype(bfloat)

    @pl.when(step >= half)
    def _():
        out_long[...] = result.astype(bfloat)


def flip(bit):
    return [(i, i ^ bit) for i in range(SHARDS)]


def across(array, bit):
    return lax.ppermute(array, "fsdp", flip(bit))


def to_replica(array):
    return lax.ppermute(array, "rep", [(0, 1), (1, 0)])


def tie(*values):
    return lax.optimization_barrier(values)


def spread(line, other):
    others = [other] + [across(piece, 2) for piece in line[1:]]
    pieces = []
    for held in zip(line, others):
        for piece in held:
            pieces += [piece, across(piece, 1)]
    return pieces


def along(shard):
    return [shard] + [across(shard, z << 2) for z in (1, 2, 3)]


def added(*terms):
    total = terms[0].astype(single)
    for term in terms[1:]:
        total = total + term.astype(single)
    return total


class Scatter:
    def __init__(self, count, keep, send):
        self.count = count
        self.keep = keep
        if count == SHARDS:
            self.came = across(send, 1)
        else:
            both = jnp.stack([keep, send]).reshape((2, 2, 4) + keep.shape[1:])
            whole = both.transpose(2, 1, 0, 3, 4).reshape(-1, keep.shape[2])
            self.share = lax.psum_scatter(whole, "fsdp", scatter_dimension=0, tiled=True)

    def over_y(self, *after):
        if self.count != SHARDS:
            return after
        self.keep, self.came, after = tie(self.keep, self.came, after)
        theirs = added(self.keep[4:], self.came[4:]).astype(bfloat)
        self.keep = added(self.keep[:4], self.came[:4]).astype(bfloat)
        theirs, after = tie(theirs, after)
        self.came = across(theirs, 2)
        return after

    def over_z(self, *after):
        if self.count != SHARDS:
            return after
        self.keep, self.came, after = tie(self.keep, self.came, after)
        slots = [added(self.keep[z], self.came[z]) for z in range(4)]
        self.keep = slots[0].astype(bfloat)
        lows, after = tie([slot.astype(bfloat) for slot in slots[1:]], after)
        self.came = [across(low, (z + 1) << 2) for z, low in enumerate(lows)]
        return after

    def over_x(self, *after):
        if self.count == SHARDS:
            terms, after = tie([self.keep] + self.came, after)
            self.share = added(*terms).astype(bfloat)
        else:
            self.share = self.share.astype(bfloat)
        self.share, after = tie(self.share, after)
        self.other = to_replica(self.share)
        return after

    def result(self):
        return added(self.share, self.other)


def shards(
    count,
    input_short,
    input_long,
    steps_short,
    steps_long,
    upstream_short,
    upstream_long,
    step_table,
    attn_gain,
    attn_shift,
    qkv_weight,
    query_bias,
    value_bias,
    out_weight,
    out_bias,
    ffn_gain,
    ffn_shift,
    up_weight,
    up_bias,
    down_weight,
    down_bias,
):
    width, rows = out_weight.shape[1], out_weight.shape[0]
    hidden = up_weight.shape[1]
    n_short, n_long = steps_short.shape[0], steps_long.shape[0]
    short = input_short.reshape(-1, width)
    long = input_long.reshape(-1, width)
    up_short = upstream_short.reshape(-1, width)
    up_long = upstream_long.reshape(-1, width)
    total = short.shape[0] + long.shape[0]
    grid = total // TILE
    half = short.shape[0] // TILE
    heads = width // HEAD_DIM
    timesteps = step_table.shape[0]

    first_shard = qkv_weight.astype(bfloat)
    up_shard = jnp.concatenate([out_weight, up_weight], axis=1).astype(bfloat)
    down_shard = down_weight.astype(bfloat)

    place = (lax.axis_index("fsdp") if count == SHARDS else jnp.int32(0)).reshape(1).astype(jnp.int32)
    owners = width // rows
    steps = jnp.concatenate([steps_short, steps_long])
    marks = steps.shape[0]
    vectors = [attn_gain, attn_shift, query_bias, value_bias, out_bias, ffn_gain, ffn_shift, down_bias]
    own = jnp.concatenate(vectors + [up_bias]).astype(bfloat)
    told = lax.all_to_all(jnp.broadcast_to(steps, (owners, marks)), "fsdp", 0, 0, tiled=True)
    if count == SHARDS:
        shard_z = along(first_shard)
        shard_y = across(first_shard, 2)
        told, shard_z, shard_y = tie(told, shard_z, shard_y)
    chosen = (told.reshape(-1, 1) == jnp.arange(timesteps, dtype=jnp.int32)).astype(bfloat)
    chosen = jnp.dot(chosen, step_table.astype(bfloat), preferred_element_type=single).astype(bfloat)
    chosen = chosen.reshape(owners, marks * rows)
    chosen = jnp.concatenate([chosen, jnp.broadcast_to(own, (owners, own.shape[0]))], axis=1)
    told = lax.all_to_all(chosen, "fsdp", 0, 0, tiled=True)
    most = (marks + 8) * rows
    told = told.astype(single)
    rest = told[:, :most].reshape(owners, marks + 8, rows).transpose(1, 0, 2).reshape(marks + 8, width)
    embed = jnp.pad(rest[:marks], ((0, 8 - marks), (0, 0)))
    smalls = rest[marks:]
    bias = told[:, most:].reshape(1, hidden)
    if count == SHARDS:
        up_shard, shard_y = tie(up_shard, shard_y)
        first_pieces = spread(shard_z, shard_y)
        up_line, others, embed, smalls, bias = tie(
            along(up_shard), [first_pieces[i] for i in (6, 10, 14)], embed, smalls, bias
        )
        first_pieces[6], first_pieces[10], first_pieces[14] = others
        up_line = jnp.stack(up_line)
        up_line, down_shard, first_pieces[-1] = tie(up_line, down_shard, first_pieces[-1])
        up_core, up_other = across(up_line, 1), across(up_line, 2)
        down_line = along(down_shard)
    else:
        first_pieces = [lax.all_gather(first_shard, "fsdp", axis=0, tiled=True)]
        up_pieces = [lax.all_gather(up_shard, "fsdp", axis=0, tiled=True)[None]]
        down_pieces = [lax.all_gather(down_shard, "fsdp", axis=0, tiled=True)[None]]
    n = len(first_pieces)
    first_specs = [resident(p.shape) for p in first_pieces]

    tile = (TILE, width)
    short_spec, long_spec = of_short(tile, half), of_long(tile, half)
    band, half_band = (BAND, width), short.shape[0] // BAND
    short_band, long_band = of_short(band, half_band), of_long(band, half_band)
    probs_short_spec = of_short((TILE // SHORT, heads // 2, 2 * SHORT, SHORT), half)
    probs_long_spec = of_long((1, heads // 2, 2 * LONG, LONG), half)
    shape = jax.ShapeDtypeStruct
    first, qkv, probs_short, probs_long, mixed = pl.pallas_call(
        functools.partial(forward_attention, half, width, n),
        grid=(grid,),
        in_specs=[on_scalars(), short_spec, long_spec, kept((8, width)), kept((8, width))] + first_specs,
        out_specs=[
            by_step(tile),
            by_step((TILE, 3 * width)),
            probs_short_spec,
            probs_long_spec,
            by_step(tile),
        ],
        out_shape=[
            shape((total, width), bfloat),
            shape((total, 3 * width), bfloat),
            shape((n_short, heads // 2, 2 * SHORT, SHORT), bfloat),
            shape((n_long, heads // 2, 2 * LONG, LONG), bfloat),
            shape((total, width), bfloat),
        ],
        scratch_shapes=[pltpu.VMEM((width, 3 * width), bfloat), pltpu.VMEM((1, 3 * width), single)],
        compiler_params=params(),
        cost_estimate=cost(2 * total * width * 3 * width * 2, total * width * 40),
        name="forward_attention",
    )(place, short, long, embed, smalls, *first_pieces)

    owners = width // rows
    if count == SHARDS:
        down_line, up_other, up_core, mixed = tie(down_line, up_other, up_core, mixed)
        up_pieces = [up_line, up_other, up_core, across(up_other, 1)]
        down_line = jnp.stack(down_line)
        down_line, up_pieces = tie(down_line, up_pieces)
        down_core, down_other = across(down_line, 1), across(down_line, 2)
    middle, second, active, slope = pl.pallas_call(
        functools.partial(forward_up, half_band, width, hidden, len(up_pieces)),
        grid=(total // BAND,),
        in_specs=[
            on_scalars(),
            short_band,
            long_band,
            kept((8, width)),
            kept((8, width)),
            kept((1, hidden)),
            by_step(band),
        ]
        + [resident(p.shape) for p in up_pieces],
        out_specs=[
            by_step(band),
            by_step(band),
            by_step((BAND, hidden)),
            by_step((BAND, hidden)),
        ],
        out_shape=[
            shape((total, width), single),
            shape((total, width), bfloat),
            shape((total, hidden), bfloat),
            shape((total, hidden), bfloat),
        ],
        scratch_shapes=[pltpu.VMEM((width, width + hidden), bfloat)],
        compiler_params=params(),
        cost_estimate=cost(2 * total * width * (width + hidden) * 2, total * width * 20),
        name="forward_up",
    )(place, short, long, embed, smalls, bias, mixed, *up_pieces)

    slots = SHARDS // 2
    whole_rows = width // SHARDS
    down_terms = pl.pallas_call(
        down_weight_back,
        grid=(hidden // width,),
        in_specs=[
            pl.BlockSpec((total, width), lambda i: (0, i)),
            kept(up_short.shape),
            kept(up_long.shape),
        ],
        out_specs=by_step((width, width)),
        out_shape=shape((hidden, width), bfloat),
        scratch_shapes=[pltpu.VMEM((total, width), bfloat)],
        compiler_params=params(),
        cost_estimate=cost(2 * total * width * hidden, total * width * 12),
        name="down_weight_back",
    )(active, up_short, up_long)
    down_share = lax.psum_scatter(down_terms, "fsdp", scatter_dimension=0, tiled=True)
    if count == SHARDS:
        down_terms, slope, down_other = tie(down_terms, slope, down_other)
        down_pieces = [down_line, down_other, down_core, across(down_other, 1)]

    hidden_grad, branch, middle_grad, mixed_grad, vectors, bias_grad = pl.pallas_call(
        functools.partial(feed_back, half_band, width, hidden, len(down_pieces)),
        grid=(total // BAND,),
        in_specs=[
            on_scalars(),
            short_band,
            long_band,
            by_step((BAND, hidden)),
            by_step(band),
            kept((8, width)),
        ]
        + [resident(p.shape) for p in [*up_pieces, *down_pieces]],
        out_specs=[
            by_step((BAND, hidden)),
            by_step(band),
            by_step(band),
            by_step(band),
            kept((8, width)),
            kept((1, hidden)),
        ],
        out_shape=[
            shape((total, hidden), bfloat),
            shape((total, width), bfloat),
            shape((total, width), single),
            shape((total, width), bfloat),
            shape((8, width), single),
            shape((1, hidden), single),
        ],
        scratch_shapes=[
            pltpu.VMEM((width, width + hidden), bfloat),
            pltpu.VMEM((hidden, width), bfloat),
            pltpu.VMEM(band, bfloat),
        ],
        compiler_params=params(),
        cost_estimate=cost(2 * total * width * (width + 2 * hidden), total * width * 30),
        name="feed_back",
    )(place, up_short, up_long, slope, middle, smalls, *up_pieces, *down_pieces)

    tiles = hidden // width
    column = lambda last: pl.BlockSpec((total, width), lambda i: (0, jnp.minimum(i, last)))
    out_block = pl.BlockSpec((slots, whole_rows, width), lambda i: (0, 0, i))
    up_keep, up_send = pl.pallas_call(
        functools.partial(weight_back, (1, tiles)),
        grid=(tiles + 1,),
        in_specs=[
            on_scalars(),
            kept((total, width)),
            kept((total, width)),
            kept((total, width)),
            pl.BlockSpec((total, width), lambda i: (0, jnp.maximum(i - 1, 0))),
        ],
        out_specs=[out_block] * 2,
        out_shape=[shape((slots, whole_rows, width + hidden), bfloat)] * 2,
        scratch_shapes=[pltpu.VMEM((width, total), bfloat)],
        compiler_params=params(),
        cost_estimate=cost(2 * total * width * (width + hidden), total * width * 20),
        name="up_weight_back",
    )(place, mixed, second, branch, hidden_grad)
    up_sum = Scatter(count, up_keep, up_send)
    (qkv,) = up_sum.over_y(qkv)

    projected_grad = pl.pallas_call(
        functools.partial(backward_attention, half, width),
        grid=(grid,),
        in_specs=[by_step((TILE, 3 * width)), by_step(tile), probs_short_spec, probs_long_spec],
        out_specs=by_step((TILE, 3 * width)),
        out_shape=shape((total, 3 * width), bfloat),
        compiler_params=params(24 << 20),
        cost_estimate=cost(2 * total * width * 3 * width * 2, total * width * 20),
        name="backward_attention",
    )(qkv, mixed_grad, probs_short, probs_long)

    qkv_keep, qkv_send = pl.pallas_call(
        functools.partial(weight_back, (3,)),
        grid=(3,),
        in_specs=[on_scalars(), kept((total, width)), column(2)],
        out_specs=[out_block] * 2,
        out_shape=[shape((slots, whole_rows, 3 * width), bfloat)] * 2,
        scratch_shapes=[pltpu.VMEM((width, total), bfloat)],
        compiler_params=params(36 << 20),
        cost_estimate=cost(2 * total * width * 3 * width, total * width * 16),
        name="qkv_weight_back",
    )(place, first, projected_grad)
    qkv_sum = Scatter(count, qkv_keep, qkv_send)
    qkv_sum.keep, middle_grad = tie(qkv_sum.keep, middle_grad)
    grad_short, grad_long, last_vectors, sums = pl.pallas_call(
        functools.partial(start_back, half_band, width, n),
        grid=(total // BAND,),
        in_specs=[
            on_scalars(),
            short_band,
            long_band,
            kept((8, width)),
            kept((8, width)),
            by_step(band),
            by_step((BAND, 3 * width)),
        ]
        + first_specs,
        out_specs=[short_band, long_band, kept((8, width)), kept((8, width))],
        out_shape=[
            shape(short.shape, bfloat),
            shape(long.shape, bfloat),
            shape((8, width), single),
            shape((8, width), single),
        ],
        scratch_shapes=[pltpu.VMEM((width, 3 * width), bfloat)],
        compiler_params=params(),
        cost_estimate=cost(2 * total * width * 3 * width, total * width * 30),
        name="start_back",
    )(place, short, long, embed, smalls, middle_grad, projected_grad, *first_pieces)
    sums, qkv_sum.keep, down_share = up_sum.over_z(sums, qkv_sum.keep, down_share)
    sums, middle = qkv_sum.over_y(sums, middle)
    owners = width // rows
    both = jnp.concatenate([vectors[:4], last_vectors[:4], sums[:marks]], axis=0)
    lines = both.shape[0]
    packed = both.reshape(lines, owners, rows).transpose(1, 0, 2).reshape(owners, lines * rows)
    own_steps = jnp.broadcast_to(steps.astype(single), (owners, marks))
    packed = jnp.concatenate([packed, bias_grad.reshape(owners, -1), own_steps], axis=1)
    packed = jnp.concatenate([packed, packed], axis=0)
    came = lax.all_to_all(packed, ("rep", "fsdp"), 0, 0, tiled=True)
    output_short, output_long = pl.pallas_call(
        functools.partial(forward_down, half_band, len(down_pieces)),
        grid=(total // BAND,),
        in_specs=[on_scalars(), by_step(band), by_step((BAND, hidden)), kept((8, width))]
        + [resident(p.shape) for p in down_pieces],
        out_specs=[short_band, long_band],
        out_shape=[shape(short.shape, bfloat), shape(long.shape, bfloat)],
        scratch_shapes=[pltpu.VMEM((hidden, width), bfloat)],
        compiler_params=params(),
        cost_estimate=cost(2 * total * width * hidden, total * width * 30),
        name="forward_down",
    )(place, middle, active, smalls, *down_pieces)

    if count == SHARDS:
        up_sum.came, qkv_sum.came, came, output_short = tie(up_sum.came, qkv_sum.came, came, output_short)
    output_short, down_share = up_sum.over_x(output_short, down_share)
    down_other = to_replica(down_share)
    output_short, came = qkv_sum.over_z(output_short, came)
    vector_sums = jnp.sum(came[:, : 8 * rows], axis=0).reshape(8, rows)
    ends = lines * rows + hidden // owners
    up_bias_grad = jnp.sum(came[:, lines * rows : ends], axis=0)
    sequence_sums = came[:, 8 * rows : lines * rows].reshape(-1, rows)
    all_steps = came[:, ends:].astype(jnp.int32).reshape(-1)
    selector = (all_steps[:, None] == jnp.arange(timesteps, dtype=jnp.int32)[None, :]).astype(single)
    table_grad = lax.dot_general(
        selector,
        sequence_sums,
        TN,
        precision=lax.Precision.HIGHEST,
        preferred_element_type=single,
    )
    down_other, up_sum.other = qkv_sum.over_x(down_other, up_sum.other)
    up_grads, qkv_weight_grad = up_sum.result(), qkv_sum.result()
    down_weight_grad = added(down_share, down_other)
    return (
        output_short.reshape(input_short.shape),
        output_long.reshape(input_long.shape),
        grad_short.reshape(input_short.shape),
        grad_long.reshape(input_long.shape),
        table_grad,
        vector_sums[4],
        vector_sums[5],
        qkv_weight_grad,
        vector_sums[6],
        vector_sums[7],
        up_grads[:, :width],
        vector_sums[2],
        vector_sums[0],
        vector_sums[1],
        up_grads[:, width:],
        up_bias_grad,
        down_weight_grad,
        vector_sums[3],
    )


def solution(mesh):
    rows = P(("rep", "fsdp"), None, None)
    steps = P(("rep", "fsdp"))
    vector, matrix, table = P("fsdp"), P("fsdp", None), P(None, "fsdp")
    weights = (
        table,
        vector,
        vector,
        matrix,
        vector,
        vector,
        matrix,
        vector,
        vector,
        vector,
        matrix,
        vector,
        matrix,
        vector,
    )
    return jax.shard_map(
        functools.partial(shards, mesh.shape["fsdp"]),
        mesh=mesh,
        in_specs=(rows, rows, steps, steps, rows, rows) + weights,
        out_specs=(rows,) * 4 + weights,
        check_vma=False,
    )
```
